32 devices in a mesh: group: 2 (over y), atom: 4 (over z), wave: 4 (over x, core).
Axes of the slice: x: 2, y: 2, z: 4, core: 2. Of those that a mesh axis runs over, the one named last changes fastest.
Arguments:
- positions: float32 [4, 3, 4096], P(None, None, ('group', 'atom')), parts along dimension 2, may hold values from 0 to 1
- charges: bfloat16 [4, 8, 4096], P(None, None, ('group', 'atom')), parts along dimension 2, may hold values from -6 to 6
- lattice: int32 [3, 2048], P(None, 'wave'), may hold values from -8 to 8, as said below
Outputs:
- potentials: float32 [4, 8, 4096], P(None, None, ('group', 'atom', 'wave')), parts along dimension 2
- forces: float32 [4, 3, 4096], P(None, None, ('group', 'atom', 'wave')), parts along dimension 2
- energy: float32 [8], P('group'), parts along dimension 0
The draws below stay inside these ranges and needn't reach their ends.
There are 2 independent parts, one for each index of `group`. The reference program is written for one: setup_inputs(seed, part) draws one part's arguments, and reference() takes and returns one part's arrays. A program takes and returns all parts, laid end to end along the dimension named above; an argument that names none is the same for every part. Nothing has to cross between parts.
Inputs may be any that keep to these rules, and one draw needn't show every extreme that they name: `lattice`: the columns are distinct nonzero integer vectors of squared length at most 64; the six vectors with one entry of magnitude 8 are always among them.
All inputs are finite; a program needn't handle non-finite values.
Results may differ from the reference program's by a relative error of at most 0.0043.
Values sent between devices are 32-bit elements; how exact they have to be, the bound alone decides.
No kernel may reach another device: no remote copies, remote signals or barrier semaphores. Data moves between devices by JAX's collectives and lax.ppermute only.
A program may use at most 64 MiB of HBM per device.

```python
import math
import jax
import jax.numpy as jnp
import numpy as np
from jax import lax

CHAN = 8
WAVES = 2048
BOX = 32
FRAMES = 4
ATOMS = 2048


def ball_table():
    steps = np.arange(-8, 9)
    first, second, third = np.meshgrid(steps, steps, steps, indexing='ij')
    first = first.reshape(-1)
    second = second.reshape(-1)
    third = third.reshape(-1)
    square = first * first + second * second + third * third
    inside = (square > 0) & (square <= 64)
    ends = inside & (square == 64) & ((np.abs(first) == 8) | (np.abs(second) == 8) | (np.abs(third) == 8))
    others = inside ^ ends
    table = np.stack([first, second, third], 0)
    return (table[:, ends].astype(np.int32), table[:, others].astype(np.int32))


def draw_lattice(key, part):
    ends, others = ball_table()
    ends = jnp.asarray(ends)
    others = jnp.asarray(others)
    pick_key = jax.random.fold_in(key, 11)
    order_key = jax.random.fold_in(key, 23)
    chosen = jax.random.permutation(pick_key, others.shape[1])[:WAVES - 6].astype(jnp.int32)
    picked = jnp.concatenate([ends, jnp.take(others, chosen, axis=1)], 1)
    order = jax.random.permutation(order_key, WAVES).astype(jnp.int32)
    return jnp.take(picked, order, axis=1).astype(jnp.int32)


def level_of(own_key, shape, split, least, top_value):
    gain = 1.0
    for position, blocks in split:
        draws = jax.random.uniform(jax.random.fold_in(jax.random.fold_in(own_key, 6), position), (blocks,), jnp.float32, least / len(split), top_value / len(split))
        gain = gain * jnp.repeat(jnp.exp(draws), shape[position] // blocks).reshape((-1,) + (1,) * (len(shape) - 1 - position))
    return gain


def noise(key, extent, scale, reach, split=(), held_as=jnp.bfloat16):
    loudness = level_of(key, extent, split, -0.22, 0.18) if split else 1.0
    entries = jax.random.normal(key, extent, jnp.float32) * scale * loudness
    return jnp.minimum(jnp.maximum(entries, -reach), reach).astype(held_as)


def setup_inputs(seed: int = 0, part: int = 0) -> dict:
    arg_keys = jax.random.split(jax.random.key(seed), 4)
    part_splits = jax.random.split(jax.random.fold_in(arg_keys[3], part), 4)
    positions = jnp.clip(1.0 * jax.random.uniform(part_splits[0], (FRAMES, 3, ATOMS), jnp.float32) ** level_of(part_splits[0], (FRAMES, 3, ATOMS), ((2, 4),), -0.2, 0.2), 0.0, 1.0)
    charges = noise(part_splits[1], (FRAMES, CHAN, ATOMS), 1.0, 6.0, ((2, 4),))
    lattice = draw_lattice(jax.random.fold_in(arg_keys[3], 71), part)
    return dict(positions=positions, charges=charges, lattice=lattice)


TWO_PI = 2.0 * math.pi
GAUSS = 256.0

def wave_weights(nvec):
    square = nvec[0] * nvec[0] + nvec[1] * nvec[1] + nvec[2] * nvec[2]
    return jnp.exp(-square / GAUSS) / square

def phase_tables(frac, nvec):
    theta = TWO_PI * (frac[0][:, None] * nvec[0][None, :] + frac[1][:, None] * nvec[1][None, :] + frac[2][:, None] * nvec[2][None, :])
    return (jnp.cos(theta).astype(jnp.bfloat16), jnp.sin(theta).astype(jnp.bfloat16))

def left_tables(real, imag, nvec, weight):
    scaled = weight[None, :] * nvec
    left_cos = jnp.concatenate([weight[None, :] * real] + [-scaled[d][None, :] * imag for d in range(3)], 0)
    left_sin = jnp.concatenate([weight[None, :] * imag] + [scaled[d][None, :] * real for d in range(3)], 0)
    return (left_cos.astype(jnp.bfloat16), left_sin.astype(jnp.bfloat16))

def atom_terms(frac, charge, nvec, left_cos, left_sin, scale_pot, scale_force):
    cosine, sine = phase_tables(frac, nvec)
    dims = (((1,), (1,)), ((), ()))
    summed = lax.dot_general(left_cos, cosine, dims, preferred_element_type=jnp.float32)
    summed = summed + lax.dot_general(left_sin, sine, dims, preferred_element_type=jnp.float32)
    chan = charge.shape[0]
    potential = scale_pot * summed[:chan]
    force = scale_force * lax.optimization_barrier(jnp.sum(summed[chan:].reshape(3, chan, -1) * charge.astype(jnp.float32)[None], axis=1))
    return jnp.concatenate([potential, force], 0)

def reference(positions, charges, lattice):
    nvec = lattice.astype(jnp.float32)
    weight = wave_weights(nvec)
    pref = 1.0 / math.sqrt(ATOMS)
    rows = math.gcd(ATOMS, 2048)
    count = ATOMS // rows

    def one_frame(inputs):
        frac, charge = inputs
        frac_blocks = frac.reshape(3, count, rows).transpose(1, 0, 2)
        charge_blocks = charge.reshape(CHAN, count, rows).transpose(1, 0, 2)

        def accumulate(carry, block):
            cosine, sine = phase_tables(block[0], nvec)
            real = carry[0] + jnp.dot(block[1], cosine, preferred_element_type=jnp.float32)
            imag = carry[1] + jnp.dot(block[1], sine, preferred_element_type=jnp.float32)
            return ((real, imag), 0)
        zeros = jnp.zeros((CHAN, WAVES), jnp.float32)
        (real, imag), _ = lax.scan(accumulate, (zeros, zeros), (frac_blocks, charge_blocks))
        energy = pref * jnp.sum(weight[None, :] * (real * real + imag * imag)) / ATOMS
        left_cos, left_sin = left_tables(real, imag, nvec, weight)

        def block_terms(block):
            return atom_terms(block[0], block[1], nvec, left_cos, left_sin, 2.0 * pref, 2.0 * TWO_PI * pref / BOX)
        terms = lax.map(block_terms, (frac_blocks, charge_blocks))
        terms = terms.transpose(1, 0, 2).reshape(CHAN + 3, ATOMS)
        return (terms, energy)
    terms, energy = lax.map(one_frame, (positions, charges))
    return (terms[:, :CHAN], terms[:, CHAN:], energy)
```

```python
import functools
import math

import jax
import jax.numpy as jnp
from jax import lax
from jax.experimental import pallas as pl
from jax.experimental.pallas import tpu as pltpu
from jax.sharding import PartitionSpec as P

BOX = 32
TWO_PI = 2.0 * math.pi
GAUSS = 256.0
TOP = 8

SIN = (3.14159265, -5.16771008, 2.55007753, -0.59829131, 0.07765766)
COS = (1.0, -4.93479283, 4.05841139, -1.33187667, 0.21968962)

NT = (((1,), (1,)), ((), ()))
NN = (((1,), (0,)), ((), ()))
TN = (((0,), (0,)), ((), ()))


def horner(coefs, u):
    value = jnp.full_like(u, coefs[-1])
    for c in coefs[-2::-1]:
        value = value * u + c
    return value


def cos_sin(turns):
    r = turns - jnp.round(turns)
    u = r * r
    s = r * horner(SIN, u)
    c = horner(COS, u)
    return 1.0 - 2.0 * (s * s), 2.0 * (s * c)


def iota(shape, dim):
    return lax.broadcasted_iota(jnp.int32, shape, dim)


def bases(x, y, z):
    k = iota(x.shape, 0)
    kf = k.astype(jnp.float32)
    out = [cos_sin(kf * v) for v in (x, y, z)]
    last = jnp.where(k < 2, x, jnp.where(k < 4, y, z))
    quarter = jnp.where((k & 1) == 1, 0.25, 0.0)
    out.append(cos_sin(TOP * last - quarter))
    return out


def weights(blocks):
    counts = jnp.zeros((64, 32), jnp.float32)
    ends = jnp.zeros((8, 128), jnp.float32)
    for block in blocks:
        n0, n1, n2 = block[0:1], block[1:2], block[2:3]
        n = n0.shape[1]
        a0, a1, a2 = jnp.abs(n0), jnp.abs(n1), jnp.abs(n2)
        one = jnp.ones_like(n0)
        zero = jnp.zeros_like(n0)

        def sgn(v):
            return jnp.where(v > 0, one, jnp.where(v < 0, -one, zero))

        s0, s1, s2 = sgn(n0), sgn(n1), sgn(n2)
        row = iota((64, n), 0)
        key = ((row // 8) * 16 + row % 8).astype(jnp.float32)
        left = jnp.where(key == a0 * 16.0 + a1, 1.0, 0.0)
        row8 = iota((8, n), 0)
        k8 = row8.astype(jnp.float32)
        hit = k8 == a2
        right = jnp.concatenate(
            [jnp.where(hit, s, 0.0) for s in (one, s1 * s2, s0 * s2, s0 * s1)], 0
        )
        counts += lax.dot_general(
            left.astype(jnp.bfloat16),
            right.astype(jnp.bfloat16),
            NT,
            preferred_element_type=jnp.float32,
        )
        size = jnp.where(row8 < 2, a0, jnp.where(row8 < 4, a1, a2))
        end = jnp.where(size == TOP, 1.0, 0.0)
        for j in range(0, n, 128):
            ends += end[:, j : j + 128]
    row = iota((64, 128), 0)
    lane = iota((64, 128), 1)
    k0, k1, k2 = row // 8, row % 8, (lane // 8) % 8
    square = (k0 * k0 + k1 * k1 + k2 * k2).astype(jnp.float32)
    some = square > 0
    safe = jnp.where(some, square, 1.0)
    gauss = jnp.where(some, jnp.exp(-safe / GAUSS) / safe, 0.0)
    source = iota((32, 128), 0)
    target = iota((32, 128), 1)
    tau = jnp.where(target < 64, 1.0, -1.0)
    out = []
    for v in range(4):
        pick = jnp.where(source == v * 8 + (target // 8) % 8, 1.0, 0.0)
        if v in (1, 2):
            pick = pick * tau
        spread = lax.dot_general(
            counts.astype(jnp.bfloat16),
            pick.astype(jnp.bfloat16),
            NN,
            preferred_element_type=jnp.float32,
        )
        out.append(gauss * spread)
    number = jnp.sum(ends, axis=1, keepdims=True)
    edge = math.exp(-TOP * TOP / GAUSS) / (TOP * TOP)
    keep = (iota((8, 128), 1) < 8) & (iota((8, 128), 0) < 6)
    return out, jnp.where(keep, edge * number, 0.0)


def spectrum(t, w, ends):
    tile = lambda j, y: t[16 * j + 8 * y : 16 * j + 8 * y + 8]
    turn = lambda v: pltpu.roll(v, 64, 1)
    out = []
    for k0 in range(8):
        w0, w1, w2, w3 = (v[8 * k0 : 8 * k0 + 8] for v in w)
        for x in range(2):
            if k0 == 0 and x == 1:
                out.append(ends * tile(1, 0))
                out.append(jnp.zeros_like(ends))
                continue
            for y in range(2):
                sy = 1.0 if y == 0 else -1.0
                sx = 1.0 if x == 0 else -1.0
                m = w0 * tile(2 * k0 + x, y) - sy * w1 * turn(tile(2 * k0 + x, 1 - y))
                if k0:
                    m = m - sx * w2 * turn(tile(2 * k0 + 1 - x, y))
                    m = m - sx * sy * w3 * tile(2 * k0 + 1 - x, 1 - y)
                out.append(m)
    return jnp.concatenate(out, 0)


def kernel(frames, chan, scale_pot, scale_force, scale_energy, count, *refs):
    shards = refs[:count]
    pot_ref, force_ref, energy_ref, a_ref, b_ref, basis = refs[count:]
    own = shards[0]
    width = own.shape[2]
    part = pot_ref.shape[2]
    first = frames * chan
    lattice_row = first + 3 * frames

    w, ends = weights([s[0, lattice_row : lattice_row + 3, :] for s in shards[:4]])

    def spread(ref, row):
        line = ref[pl.ds(row, 1), :]
        return jnp.broadcast_to(line, (8, line.shape[1]))

    def fill(shard, index, frame, base, slot):
        block = shard.at[index]
        x, y, z = (spread(block, first + 3 * frame + d) for d in range(3))
        (xc, xs), (yc, ys), (zc, zs), (ec, _) = bases(x, y, z)
        q = block[pl.ds(chan * frame, chan), :]
        table = basis.at[slot]
        table[0:8] = xc
        table[8:16] = xs
        table[16:24] = zc
        table[24:32] = zs
        columns = pl.ds(base, width)
        for k0 in range(8):
            for kind in range(2):
                j = 2 * k0 + kind
                if j == 1:
                    value = jnp.concatenate([ec, ec], 0)
                else:
                    f = spread(table, 8 * kind + k0)
                    value = jnp.concatenate([f * yc, f * ys], 0)
                a_ref[frame % 2, 16 * j : 16 * j + 16, columns] = value.astype(jnp.bfloat16)
        for kind in range(2):
            for k in range(0, 8, 2):
                j = 8 * kind + k
                value = jnp.concatenate(
                    [spread(table, 16 + j) * q, spread(table, 17 + j) * q], 0
                )
                b_ref[frame % 2, 8 * j : 8 * j + 16, columns] = value.astype(jnp.bfloat16)

    start = pl.multiple_of(lax.axis_index("wave") * part, part)
    block = own[0, :, pl.ds(start, part)]
    for frame in range(frames):
        at = 0
        slot = 0
        for shard in shards:
            if shard.shape[0] == 1:
                fill(shard, 0, frame, at, slot % 2)
            else:

                @pl.loop(0, shard.shape[0])
                def _(i, at=at, shard=shard):
                    fill(shard, i, frame, pl.multiple_of(at + i * width, width), 0)

            at += width * shard.shape[0]
            slot += 1
        t = lax.dot_general(
            a_ref[frame % 2], b_ref[frame % 2], NT, preferred_element_type=jnp.float32
        )
        m = spectrum(t, w, ends)
        energy_ref[frame] = scale_energy * jnp.sum(t * m)

        line = first + 3 * frame
        x, y, z = (
            jnp.broadcast_to(block[line + d : line + d + 1], (8, part)) for d in range(3)
        )
        (xc, xs), (yc, ys), (zc, zs), (ec, es) = bases(x, y, z)
        q = block[chan * frame : chan * frame + chan]
        row = lambda v, k: jnp.broadcast_to(v[k : k + 1], v.shape)
        xrow = [(row(xc, k), row(xs, k)) for k in range(8)]
        zrow = [[row(v, k) for k in range(8)] for v in (zc, zs)]
        atoms = []
        for k0 in range(8):
            for kind in range(2):
                if k0 == 0 and kind == 1:
                    atoms += [ec, jnp.zeros_like(ec)]
                else:
                    atoms += [xrow[k0][kind] * yc, xrow[k0][kind] * ys]
        atoms = jnp.concatenate(atoms, 0)
        loads = jnp.concatenate([v * q for kind in zrow for v in kind], 0)
        h = lax.dot_general(
            m, loads, NN, precision=lax.Precision.HIGHEST, preferred_element_type=jnp.float32
        )
        u = lax.dot_general(
            m, atoms, TN, precision=lax.Precision.HIGHEST, preferred_element_type=jnp.float32
        )
        pot = jnp.zeros_like(q)
        dz = jnp.zeros_like(q)
        for k in range(8):
            uc = u[8 * k : 8 * k + 8]
            us = u[64 + 8 * k : 72 + 8 * k]
            pot = pot + zrow[0][k] * uc + zrow[1][k] * us
            if k:
                dz = dz + float(k) * (zrow[0][k] * us - zrow[1][k] * uc)
        pot_ref[frame] = scale_pot * pot
        dx = jnp.zeros_like(q)
        gc = jnp.zeros_like(q)
        gs = jnp.zeros_like(q)
        for k0 in range(8):
            parts = []
            for kind in range(2):
                if k0 == 0 and kind == 1:
                    continue
                j = 2 * k0 + kind
                hc = h[16 * j : 16 * j + 8]
                hs = h[16 * j + 8 : 16 * j + 16]
                parts.append(hc * yc + hs * ys)
                gc = gc + xrow[k0][kind] * hc
                gs = gs + xrow[k0][kind] * hs
            if k0:
                dx = dx + float(k0) * (xrow[k0][0] * parts[1] - xrow[k0][1] * parts[0])
        k1 = iota(q.shape, 0).astype(jnp.float32)
        dy = k1 * (yc * gs - ys * gc)
        edge = -float(TOP) * es * h[16:24]
        total = lambda v: jnp.sum(v, axis=0, keepdims=True)
        fx = total(dx) + edge[0:1] + edge[1:2]
        fy = total(dy) + edge[2:3] + edge[3:4]
        fz = total(dz * q) + edge[4:5] + edge[5:6]
        force_ref[frame] = -scale_force * jnp.concatenate([fx, fy, fz], 0)


def per_device(positions, charges, lattice):
    frames, chan, width = charges.shape
    rows, columns = lax.axis_size("atom"), lax.axis_size("wave")
    atoms = width * rows
    pref = 1.0 / math.sqrt(atoms)
    packed = jnp.concatenate(
        [
            charges.astype(jnp.float32).reshape(frames * chan, width),
            positions.reshape(frames * 3, width),
            lattice.astype(jnp.float32),
        ],
        0,
    )
    shift = {0: 0, 1: 2, 2: 3, 3: 1}
    shards = [packed]
    for k in range(1, rows):
        pairs = []
        for a in range(rows):
            for b in range(columns):
                pairs.append((a * columns + b, (a ^ k) * columns + (b ^ shift[k % 4])))
        shards.append(lax.ppermute(packed, ("atom", "wave"), pairs))
    head = [s[None] for s in shards[:4]]
    if rows > 4:
        head.append(jnp.stack(shards[4:]))
    part = width // columns
    body = functools.partial(
        kernel,
        frames,
        chan,
        2.0 * pref,
        2.0 * TWO_PI * pref / BOX,
        pref / atoms,
        len(head),
    )
    return pl.pallas_call(
        body,
        out_shape=(
            jax.ShapeDtypeStruct((frames, chan, part), jnp.float32),
            jax.ShapeDtypeStruct((frames, 3, part), jnp.float32),
            jax.ShapeDtypeStruct((frames,), jnp.float32),
        ),
        in_specs=[pl.BlockSpec(memory_space=pltpu.VMEM)] * len(head),
        out_specs=(
            pl.BlockSpec(memory_space=pltpu.VMEM),
            pl.BlockSpec(memory_space=pltpu.VMEM),
            pl.BlockSpec(memory_space=pltpu.SMEM),
        ),
        scratch_shapes=[
            pltpu.VMEM((2, 256, atoms), jnp.bfloat16),
            pltpu.VMEM((2, 128, atoms), jnp.bfloat16),
            pltpu.VMEM((2, 32, width), jnp.float32),
        ],
        compiler_params=pltpu.CompilerParams(vmem_limit_bytes=56 * 2**20),
    )(*head)


def solution(mesh):
    return jax.shard_map(
        per_device,
        mesh=mesh,
        in_specs=(
            P(None, None, ("group", "atom")),
            P(None, None, ("group", "atom")),
            P(None, "wave"),
        ),
        out_specs=(
            P(None, None, ("group", "atom", "wave")),
            P(None, None, ("group", "atom", "wave")),
            P("group"),
        ),
        check_vma=False,
    )
```

```python
import functools
import math

import jax
import jax.numpy as jnp
from jax import lax
from jax.experimental import pallas as pl
from jax.experimental.pallas import tpu as pltpu
from jax.sharding import PartitionSpec as P

BOX = 32
TWO_PI = 2.0 * math.pi
GAUSS = 256.0
TOP = 8

SIN = (3.14159265, -5.16771008, 2.55007753, -0.59829131, 0.07765766)
COS = (1.0, -4.93479283, 4.05841139, -1.33187667, 0.21968962)

NT = (((1,), (1,)), ((), ()))
NN = (((1,), (0,)), ((), ()))
TN = (((0,), (0,)), ((), ()))


def horner(coefs, u):
    value = jnp.full_like(u, coefs[-1])
    for c in coefs[-2::-1]:
        value = value * u + c
    return value


def cos_sin(turns):
    r = turns - jnp.round(turns)
    u = r * r
    s = r * horner(SIN, u)
    c = horner(COS, u)
    return 1.0 - 2.0 * (s * s), 2.0 * (s * c)


def iota(shape, dim):
    return lax.broadcasted_iota(jnp.int32, shape, dim)


def bases(x, y, z):
    k = iota(x.shape, 0)
    kf = k.astype(jnp.float32)
    out = [cos_sin(kf * v) for v in (x, y, z)]
    last = jnp.where(k < 2, x, jnp.where(k < 4, y, z))
    quarter = jnp.where((k & 1) == 1, 0.25, 0.0)
    out.append(cos_sin(TOP * last - quarter))
    return out


def weights(blocks):
    counts = jnp.zeros((64, 32), jnp.float32)
    ends = jnp.zeros((8, 128), jnp.float32)
    for block in blocks:
        n0, n1, n2 = block
        n = n0.shape[1]
        a0, a1, a2 = jnp.abs(n0), jnp.abs(n1), jnp.abs(n2)
        one = jnp.ones_like(n0)
        zero = jnp.zeros_like(n0)

        def sgn(v):
            return jnp.where(v > 0, one, jnp.where(v < 0, -one, zero))

        s0, s1, s2 = sgn(n0), sgn(n1), sgn(n2)
        row = iota((64, n), 0)
        key = ((row // 8) * 16 + row % 8).astype(jnp.float32)
        left = jnp.where(key == a0 * 16.0 + a1, 1.0, 0.0)
        row8 = iota((8, n), 0)
        k8 = row8.astype(jnp.float32)
        hit = k8 == a2
        right = jnp.concatenate(
            [jnp.where(hit, s, 0.0) for s in (one, s1 * s2, s0 * s2, s0 * s1)], 0
        )
        counts += lax.dot_general(
            left.astype(jnp.bfloat16),
            right.astype(jnp.bfloat16),
            NT,
            preferred_element_type=jnp.float32,
        )
        size = jnp.where(row8 < 2, a0, jnp.where(row8 < 4, a1, a2))
        end = jnp.where(size == TOP, 1.0, 0.0)
        for j in range(0, n, 128):
            ends += end[:, j : j + 128]
    row = iota((64, 128), 0)
    lane = iota((64, 128), 1)
    k0, k1, k2 = row // 8, row % 8, (lane // 8) % 8
    square = (k0 * k0 + k1 * k1 + k2 * k2).astype(jnp.float32)
    some = square > 0
    safe = jnp.where(some, square, 1.0)
    gauss = jnp.where(some, jnp.exp(-safe / GAUSS) / safe, 0.0)
    source = iota((32, 128), 0)
    target = iota((32, 128), 1)
    tau = jnp.where(target < 64, 1.0, -1.0)
    out = []
    for v in range(4):
        pick = jnp.where(source == v * 8 + (target // 8) % 8, 1.0, 0.0)
        if v in (1, 2):
            pick = pick * tau
        spread = lax.dot_general(
            counts.astype(jnp.bfloat16),
            pick.astype(jnp.bfloat16),
            NN,
            preferred_element_type=jnp.float32,
        )
        out.append(gauss * spread)
    number = jnp.sum(ends, axis=1, keepdims=True)
    edge = math.exp(-TOP * TOP / GAUSS) / (TOP * TOP)
    keep = (iota((8, 128), 1) < 8) & (iota((8, 128), 0) < 6)
    return out, jnp.where(keep, edge * number, 0.0)


def spectrum(t, w, ends):
    tile = lambda j, y: t[16 * j + 8 * y : 16 * j + 8 * y + 8]
    turn = lambda v: pltpu.roll(v, 64, 1)
    out = []
    for k0 in range(8):
        w0, w1, w2, w3 = (v[8 * k0 : 8 * k0 + 8] for v in w)
        for x in range(2):
            if k0 == 0 and x == 1:
                out.append(ends * tile(1, 0))
                out.append(jnp.zeros_like(ends))
                continue
            for y in range(2):
                sy = 1.0 if y == 0 else -1.0
                sx = 1.0 if x == 0 else -1.0
                m = w0 * tile(2 * k0 + x, y) - sy * w1 * turn(tile(2 * k0 + x, 1 - y))
                if k0:
                    m = m - sx * w2 * turn(tile(2 * k0 + 1 - x, y))
                    m = m - sx * sy * w3 * tile(2 * k0 + 1 - x, 1 - y)
                out.append(m)
    return jnp.concatenate(out, 0)


def lines(block, first, tiles):
    return jnp.concatenate([block[first + t : first + t + 1] for t in range(tiles)], 1)


def tall(line):
    return jnp.broadcast_to(line, (8, line.shape[1]))


def pack_kernel(half, tiles, pos_ref, charge_ref, lattice_ref, own_ref, other_ref):
    mine = lax.rem(lax.axis_index("wave"), 2)
    chan = charge_ref.shape[1]
    cut = lambda t: slice(128 * t, 128 * t + 128)
    for out, side in ((own_ref, mine), (other_ref, 1 - mine)):
        row = 0
        for f in range(half):
            q = charge_ref[side * half + f].astype(jnp.float32)
            for t in range(tiles):
                out[row : row + chan, :] = q[:, cut(t)]
                row += chan
        for f in range(half):
            for d in range(3):
                line = pos_ref[d, pl.ds(side * half + f, 1), :]
                for t in range(tiles):
                    out[row : row + 1, :] = line[:, cut(t)]
                    row += 1
        lattice = lattice_ref[...].astype(jnp.float32)
        for d in range(3):
            for t in range(tiles):
                out[row : row + 1, :] = lattice[d : d + 1, cut(t)]
                row += 1


def kernel(half, chan, tiles, scale_pot, scale_force, scale_energy, count, *refs):
    shards = refs[:count]
    mine_ref, send_ref, a_ref, b_ref, basis = refs[count:]
    own = shards[0]
    width = 128 * tiles
    first = half * tiles * chan
    lattice_row = first + 3 * half * tiles

    blocks = []
    for s in shards[:4]:
        v = s[0, lattice_row : lattice_row + 3 * tiles, :]
        blocks.append([lines(v, d * tiles, tiles) for d in range(3)])
    w, ends = weights(blocks)

    def spread(ref, row):
        return tall(ref[pl.ds(row, 1), :])

    def fill(shard, index, frame, base, slot):
        block = shard.at[index]
        x, y, z = (
            jnp.concatenate(
                [spread(block, first + (frame * 3 + d) * tiles + t) for t in range(tiles)], 1
            )
            for d in range(3)
        )
        (xc, xs), (yc, ys), (zc, zs), (ec, _) = bases(x, y, z)
        q = jnp.concatenate(
            [block[pl.ds((frame * tiles + t) * chan, chan), :] for t in range(tiles)], 1
        )
        table = basis.at[slot]
        table[0:8] = xc
        table[8:16] = xs
        table[16:24] = zc
        table[24:32] = zs
        columns = pl.ds(base, width)
        for k0 in range(8):
            for kind in range(2):
                j = 2 * k0 + kind
                if j == 1:
                    value = jnp.concatenate([ec, ec], 0)
                else:
                    f = spread(table, 8 * kind + k0)
                    value = jnp.concatenate([f * yc, f * ys], 0)
                a_ref[frame % 2, 16 * j : 16 * j + 16, columns] = value.astype(jnp.bfloat16)
        for kind in range(2):
            for k in range(0, 8, 2):
                j = 8 * kind + k
                value = jnp.concatenate(
                    [spread(table, 16 + j) * q, spread(table, 17 + j) * q], 0
                )
                b_ref[frame % 2, 8 * j : 8 * j + 16, columns] = value.astype(jnp.bfloat16)

    here = lax.axis_index("wave")
    pair = (here, here + 1 - 2 * lax.rem(here, 2))
    for frame in range(half):
        at = 0
        slot = 0
        for shard in shards:
            if shard.shape[0] == 1:
                fill(shard, 0, frame, at, slot % 2)
            else:

                @pl.loop(0, shard.shape[0])
                def _(i, at=at, shard=shard):
                    fill(shard, i, frame, pl.multiple_of(at + i * width, width), 0)

            at += width * shard.shape[0]
            slot += 1
        t = lax.dot_general(
            a_ref[frame % 2], b_ref[frame % 2], NT, preferred_element_type=jnp.float32
        )
        m = spectrum(t, w, ends)
        energy = scale_energy * jnp.sum(jnp.sum(t * m, 0, keepdims=True), 1, keepdims=True)

        block = own.at[0]
        x, y, z = (
            jnp.concatenate(
                [spread(block, first + (frame * 3 + d) * tiles + p) for p in pair], 1
            )
            for d in range(3)
        )
        (xc, xs), (yc, ys), (zc, zs), (ec, es) = bases(x, y, z)
        q = jnp.concatenate(
            [
                block[pl.ds(pl.multiple_of((frame * tiles + p) * chan, chan), chan), :]
                for p in pair
            ],
            1,
        )
        row = lambda v, k: jnp.broadcast_to(v[k : k + 1], v.shape)
        xrow = [(row(xc, k), row(xs, k)) for k in range(8)]
        zrow = [[row(v, k) for k in range(8)] for v in (zc, zs)]
        atoms = []
        for k0 in range(8):
            for kind in range(2):
                if k0 == 0 and kind == 1:
                    atoms += [ec, jnp.zeros_like(ec)]
                else:
                    atoms += [xrow[k0][kind] * yc, xrow[k0][kind] * ys]
        atoms = jnp.concatenate(atoms, 0)
        loads = jnp.concatenate([v * q for kind in zrow for v in kind], 0)
        h = lax.dot_general(
            m, loads, NN, precision=lax.Precision.HIGHEST, preferred_element_type=jnp.float32
        )
        u = lax.dot_general(
            m, atoms, TN, precision=lax.Precision.HIGHEST, preferred_element_type=jnp.float32
        )
        pot = jnp.zeros_like(q)
        dz = jnp.zeros_like(q)
        for k in range(8):
            uc = u[8 * k : 8 * k + 8]
            us = u[64 + 8 * k : 72 + 8 * k]
            pot = pot + zrow[0][k] * uc + zrow[1][k] * us
            if k:
                dz = dz + float(k) * (zrow[0][k] * us - zrow[1][k] * uc)
        dx = jnp.zeros_like(q)
        gc = jnp.zeros_like(q)
        gs = jnp.zeros_like(q)
        for k0 in range(8):
            parts = []
            for kind in range(2):
                if k0 == 0 and kind == 1:
                    continue
                j = 2 * k0 + kind
                hc = h[16 * j : 16 * j + 8]
                hs = h[16 * j + 8 : 16 * j + 16]
                parts.append(hc * yc + hs * ys)
                gc = gc + xrow[k0][kind] * hc
                gs = gs + xrow[k0][kind] * hs
            if k0:
                dx = dx + float(k0) * (xrow[k0][0] * parts[1] - xrow[k0][1] * parts[0])
        k1 = iota(q.shape, 0).astype(jnp.float32)
        dy = k1 * (yc * gs - ys * gc)
        edge = -float(TOP) * es * h[16:24]
        total = lambda v: jnp.sum(v, axis=0, keepdims=True)
        fx = total(dx) + edge[0:1] + edge[1:2]
        fy = total(dy) + edge[2:3] + edge[3:4]
        fz = total(dz * q) + edge[4:5] + edge[5:6]
        pot = scale_pot * pot
        forces = [-scale_force * v for v in (fx, fy, fz)]
        for out, cut in ((mine_ref, slice(0, 128)), (send_ref, slice(128, 256))):
            out[chan * frame : chan * frame + chan, :] = pot[:, cut]
            for d in range(3):
                at = half * chan + 3 * frame + d
                out[at : at + 1, :] = forces[d][:, cut]
            at = half * (chan + 3) + frame
            out[at : at + 1, :] = jnp.broadcast_to(energy, (1, 128))


def join_kernel(half, chan, mine_ref, theirs_ref, pot_ref, force_ref, energy_ref):
    side = lax.rem(lax.axis_index("wave"), 2)
    for ref, which in ((mine_ref, side), (theirs_ref, 1 - side)):
        for f in range(half):
            to = which * half + f
            pot_ref[to] = ref[chan * f : chan * f + chan, :]
            for d in range(3):
                at = half * chan + 3 * f + d
                force_ref[d, pl.ds(to, 1), :] = ref[at : at + 1, :]
            energy_ref[to] = ref[half * (chan + 3) + f, 0]


VMEM = pl.BlockSpec(memory_space=pltpu.VMEM)
SMEM = pl.BlockSpec(memory_space=pltpu.SMEM)


def per_device(positions, charges, lattice):
    frames, chan, width = charges.shape
    rows, columns = lax.axis_size("atom"), lax.axis_size("wave")
    atoms = width * rows
    pref = 1.0 / math.sqrt(atoms)
    half = frames // 2
    tiles = width // 128
    assert width // columns == 128 and columns == 4 and rows % 4 == 0
    size = -(-(half * tiles * (chan + 3) + 3 * tiles) // 8) * 8
    packed = jax.ShapeDtypeStruct((size, 128), jnp.float32)
    own, other = pl.pallas_call(
        functools.partial(pack_kernel, half, tiles),
        out_shape=(packed, packed),
        in_specs=[VMEM] * 3,
        out_specs=(VMEM, VMEM),
        compiler_params=pltpu.CompilerParams(vmem_limit_bytes=4 * 2**20),
    )(positions.transpose(1, 0, 2), charges, lattice)
    shift = {0: 0, 1: 2, 2: 3, 3: 1}
    shards = [own]
    for k in range(1, rows):
        pairs = []
        for a in range(rows):
            for b in range(columns):
                pairs.append((a * columns + b, (a ^ k) * columns + (b ^ shift[k % 4])))
        shards.append(
            lax.ppermute(other if shift[k % 4] & 1 else own, ("atom", "wave"), pairs)
        )
    head = [s[None] for s in shards[:4]]
    if rows > 4:
        head.append(jnp.stack(shards[4:]))
    result = -(-half * (chan + 4) // 8) * 8
    body = functools.partial(
        kernel,
        half,
        chan,
        tiles,
        2.0 * pref,
        2.0 * TWO_PI * pref / BOX,
        pref / atoms,
        len(head),
    )
    piece = jax.ShapeDtypeStruct((result, 128), jnp.float32)
    mine, send = pl.pallas_call(
        body,
        out_shape=(piece, piece),
        in_specs=[VMEM] * len(head),
        out_specs=(VMEM, VMEM),
        scratch_shapes=[
            pltpu.VMEM((2, 256, atoms), jnp.bfloat16),
            pltpu.VMEM((2, 128, atoms), jnp.bfloat16),
            pltpu.VMEM((2, 32, width), jnp.float32),
        ],
        compiler_params=pltpu.CompilerParams(vmem_limit_bytes=(32 if rows > 4 else 16) * 2**20),
    )(*head)
    theirs = lax.ppermute(send, "wave", [(b, b ^ 1) for b in range(columns)])
    pot, force, energy = pl.pallas_call(
        functools.partial(join_kernel, half, chan),
        out_shape=(
            jax.ShapeDtypeStruct((frames, chan, 128), jnp.float32),
            jax.ShapeDtypeStruct((3, frames, 128), jnp.float32),
            jax.ShapeDtypeStruct((frames,), jnp.float32),
        ),
        in_specs=[VMEM, VMEM],
        out_specs=(VMEM, VMEM, SMEM),
        compiler_params=pltpu.CompilerParams(vmem_limit_bytes=4 * 2**20),
    )(mine, theirs)
    return pot, force.transpose(1, 0, 2), energy


def solution(mesh):
    return jax.shard_map(
        per_device,
        mesh=mesh,
        in_specs=(
            P(None, None, ("group", "atom")),
            P(None, None, ("group", "atom")),
            P(None, "wave"),
        ),
        out_specs=(
            P(None, None, ("group", "atom", "wave")),
            P(None, None, ("group", "atom", "wave")),
            P("group"),
        ),
        check_vma=False,
    )
```

```python
import functools
import math

import jax
import jax.numpy as jnp
from jax import lax
from jax.experimental import pallas as pl
from jax.experimental.pallas import tpu as pltpu
from jax.sharding import PartitionSpec as P

BOX = 32
TWO_PI = 2.0 * math.pi
GAUSS = 256.0
TOP = 8

SIN = (3.14159265, -5.16771008, 2.55007753, -0.59829131, 0.07765766)
COS = (1.0, -4.93479283, 4.05841139, -1.33187667, 0.21968962)

NT = (((1,), (1,)), ((), ()))
NN = (((1,), (0,)), ((), ()))
TN = (((0,), (0,)), ((), ()))


def horner(coefs, u):
    value = jnp.full_like(u, coefs[-1])
    for c in coefs[-2::-1]:
        value = value * u + c
    return value


def cos_sin(turns):
    r = turns - jnp.round(turns)
    u = r * r
    s = r * horner(SIN, u)
    c = horner(COS, u)
    return 1.0 - 2.0 * (s * s), 2.0 * (s * c)


def iota(shape, dim):
    return lax.broadcasted_iota(jnp.int32, shape, dim)


def bases(x, y, z):
    k = iota(x.shape, 0)
    kf = k.astype(jnp.float32)
    out = [cos_sin(kf * v) for v in (x, y, z)]
    last = jnp.where(k < 2, x, jnp.where(k < 4, y, z))
    quarter = jnp.where((k & 1) == 1, 0.25, 0.0)
    out.append(cos_sin(TOP * last - quarter))
    return out


def weights(blocks):
    counts = jnp.zeros((64, 32), jnp.float32)
    ends = jnp.zeros((8, 128), jnp.float32)
    for block in blocks:
        n0, n1, n2 = block
        n = n0.shape[1]
        a0, a1, a2 = jnp.abs(n0), jnp.abs(n1), jnp.abs(n2)
        one = jnp.ones_like(n0)
        zero = jnp.zeros_like(n0)

        def sgn(v):
            return jnp.where(v > 0, one, jnp.where(v < 0, -one, zero))

        s0, s1, s2 = sgn(n0), sgn(n1), sgn(n2)
        row = iota((64, n), 0)
        key = ((row // 8) * 16 + row % 8).astype(jnp.float32)
        left = jnp.where(key == a0 * 16.0 + a1, 1.0, 0.0)
        row8 = iota((8, n), 0)
        k8 = row8.astype(jnp.float32)
        hit = k8 == a2
        right = jnp.concatenate(
            [jnp.where(hit, s, 0.0) for s in (one, s1 * s2, s0 * s2, s0 * s1)], 0
        )
        counts += lax.dot_general(
            left.astype(jnp.bfloat16),
            right.astype(jnp.bfloat16),
            NT,
            preferred_element_type=jnp.float32,
        )
        size = jnp.where(row8 < 2, a0, jnp.where(row8 < 4, a1, a2))
        end = jnp.where(size == TOP, 1.0, 0.0)
        for j in range(0, n, 128):
            ends += end[:, j : j + 128]
    row = iota((64, 128), 0)
    lane = iota((64, 128), 1)
    k0, k1, k2 = row // 8, row % 8, (lane // 8) % 8
    square = (k0 * k0 + k1 * k1 + k2 * k2).astype(jnp.float32)
    some = square > 0
    safe = jnp.where(some, square, 1.0)
    gauss = jnp.where(some, jnp.exp(-safe / GAUSS) / safe, 0.0)
    source = iota((32, 128), 0)
    target = iota((32, 128), 1)
    tau = jnp.where(target < 64, 1.0, -1.0)
    out = []
    for v in range(4):
        pick = jnp.where(source == v * 8 + (target // 8) % 8, 1.0, 0.0)
        if v in (1, 2):
            pick = pick * tau
        spread = lax.dot_general(
            counts.astype(jnp.bfloat16),
            pick.astype(jnp.bfloat16),
            NN,
            preferred_element_type=jnp.float32,
        )
        out.append(gauss * spread)
    number = jnp.sum(ends, axis=1, keepdims=True)
    edge = math.exp(-TOP * TOP / GAUSS) / (TOP * TOP)
    keep = (iota((8, 128), 1) < 8) & (iota((8, 128), 0) < 6)
    return out, jnp.where(keep, edge * number, 0.0)


def spectrum(t, w, ends):
    tile = lambda j, y: t[16 * j + 8 * y : 16 * j + 8 * y + 8]
    turn = lambda v: pltpu.roll(v, 64, 1)
    out = []
    for k0 in range(8):
        w0, w1, w2, w3 = (v[8 * k0 : 8 * k0 + 8] for v in w)
        for x in range(2):
            if k0 == 0 and x == 1:
                out.append(ends * tile(1, 0))
                out.append(jnp.zeros_like(ends))
                continue
            for y in range(2):
                sy = 1.0 if y == 0 else -1.0
                sx = 1.0 if x == 0 else -1.0
                m = w0 * tile(2 * k0 + x, y) - sy * w1 * turn(tile(2 * k0 + x, 1 - y))
                if k0:
                    m = m - sx * w2 * turn(tile(2 * k0 + 1 - x, y))
                    m = m - sx * sy * w3 * tile(2 * k0 + 1 - x, 1 - y)
                out.append(m)
    return jnp.concatenate(out, 0)


def lines(block, first, tiles):
    return jnp.concatenate([block[first + t : first + t + 1] for t in range(tiles)], 1)


def tall(line):
    return jnp.broadcast_to(line, (8, line.shape[1]))


def pack_kernel(
    half, tiles, pos_hbm, charge_hbm, lattice_hbm, full_ref, own_ref, wave_ref, pos_ref, charge_ref, lattice_ref, sem
):
    copies = [
        pltpu.make_async_copy(a, b, sem.at[i])
        for i, (a, b) in enumerate(
            ((charge_hbm, charge_ref), (pos_hbm, pos_ref), (lattice_hbm, lattice_ref))
        )
    ]
    for c in copies:
        c.start()
    for c in copies:
        c.wait()
    mine = lax.rem(lax.axis_index("wave"), 2)
    chan = charge_ref.shape[1]
    cut = lambda t: slice(128 * t, 128 * t + 128)
    row = 0
    for side, outs in ((mine, (full_ref, own_ref)), (1 - mine, (full_ref,))):
        for f in range(half):
            q = charge_ref[side * half + f].astype(jnp.float32)
            for t in range(tiles):
                for out in outs:
                    out[row : row + chan, :] = q[:, cut(t)]
                row += chan
        for f in range(half):
            for d in range(3):
                line = pos_ref[d, pl.ds(side * half + f, 1), :]
                for t in range(tiles):
                    for out in outs:
                        out[row : row + 1, :] = line[:, cut(t)]
                    row += 1
    lattice = lattice_ref[...].astype(jnp.float32)
    for d in range(3):
        for t in range(tiles):
            row = d * tiles + t
            wave_ref[row : row + 1, :] = lattice[d : d + 1, cut(t)]


def spread(ref, row):
    return tall(ref[pl.ds(row, 1), :])


def place(block, frame, first, picks):
    return [
        jnp.concatenate(
            [spread(block, first + (frame * 3 + d) * picks[0] + t) for t in picks[1]], 1
        )
        for d in range(3)
    ]


def fill(block, chan, tiles, half, frame, a_ref, b_ref, table, base):
    x, y, z = place(block, frame, half * tiles * chan, (tiles, range(tiles)))
    (xc, xs), (yc, ys), (zc, zs), (ec, _) = bases(x, y, z)
    q = jnp.concatenate(
        [block[pl.ds((frame * tiles + t) * chan, chan), :] for t in range(tiles)], 1
    )
    table[0:8] = xc
    table[8:16] = xs
    table[16:24] = zc
    table[24:32] = zs
    columns = pl.ds(base, 128 * tiles)
    for k0 in range(8):
        for kind in range(2):
            j = 2 * k0 + kind
            if j == 1:
                value = jnp.concatenate([ec, ec], 0)
            else:
                f = spread(table, 8 * kind + k0)
                value = jnp.concatenate([f * yc, f * ys], 0)
            a_ref[16 * j : 16 * j + 16, columns] = value.astype(jnp.bfloat16)
    for kind in range(2):
        for k in range(0, 8, 2):
            j = 8 * kind + k
            value = jnp.concatenate([spread(table, 16 + j) * q, spread(table, 17 + j) * q], 0)
            b_ref[8 * j : 8 * j + 16, columns] = value.astype(jnp.bfloat16)


def sums(blocks, rest, half, chan, tiles, frame, a_ref, b_ref, basis):
    width = 128 * tiles
    a, b = a_ref.at[frame % 2], b_ref.at[frame % 2]
    for slot, block in enumerate(blocks):
        fill(block, chan, tiles, half, frame, a, b, basis.at[slot % 2], slot * width)
    for ref in rest:

        @pl.loop(0, ref.shape[0])
        def _(i):
            base = pl.multiple_of((i + len(blocks)) * width, width)
            fill(ref.at[i], chan, tiles, half, frame, a, b, basis.at[0], base)

    return lax.dot_general(a[...], b[...], NT, preferred_element_type=jnp.float32)


def sums_kernel(half, chan, tiles, count, more, *refs):
    blocks, rest = refs[:count], refs[count : count + more]
    t_ref, a_ref, b_ref, basis = refs[count + more :]
    for frame in range(half):
        t_ref[frame] = sums(blocks, rest, half, chan, tiles, frame, a_ref, b_ref, basis)


def kernel(half, chan, tiles, scale_pot, scale_force, scale_energy, *refs):
    own, waves, across, t_ref, u_ref, pass_ref = refs[:6]
    mine_ref, send_ref, a_ref, b_ref, basis = refs[6:]
    width = 128 * tiles
    size = half * tiles * (chan + 3)

    blocks = []
    for ref, at in (
        (waves, 0),
        (across, 0),
        (pass_ref, size),
        (pass_ref, size + 16),
    ):
        v = ref[at : at + 3 * tiles, :]
        blocks.append([lines(v, d * tiles, tiles) for d in range(3)])
    w, ends = weights(blocks)

    here = lax.axis_index("wave")
    pair = (here, here + 1 - 2 * lax.rem(here, 2))
    for frame in range(half):
        t = t_ref[frame] + u_ref[frame]
        t = t + sums((pass_ref,), (), half, chan, tiles, frame, a_ref, b_ref, basis)
        m = spectrum(t, w, ends)
        energy = scale_energy * jnp.sum(jnp.sum(t * m, 0, keepdims=True), 1, keepdims=True)

        x, y, z = place(own, frame, half * tiles * chan, (tiles, pair))
        (xc, xs), (yc, ys), (zc, zs), (ec, es) = bases(x, y, z)
        q = jnp.concatenate(
            [
                own[pl.ds(pl.multiple_of((frame * tiles + p) * chan, chan), chan), :]
                for p in pair
            ],
            1,
        )
        row = lambda v, k: jnp.broadcast_to(v[k : k + 1], v.shape)
        xrow = [(row(xc, k), row(xs, k)) for k in range(8)]
        zrow = [[row(v, k) for k in range(8)] for v in (zc, zs)]
        atoms = []
        for k0 in range(8):
            for kind in range(2):
                if k0 == 0 and kind == 1:
                    atoms += [ec, jnp.zeros_like(ec)]
                else:
                    atoms += [xrow[k0][kind] * yc, xrow[k0][kind] * ys]
        atoms = jnp.concatenate(atoms, 0)
        loads = jnp.concatenate([v * q for kind in zrow for v in kind], 0)
        h = lax.dot_general(
            m, loads, NN, precision=lax.Precision.HIGHEST, preferred_element_type=jnp.float32
        )
        u = lax.dot_general(
            m, atoms, TN, precision=lax.Precision.HIGHEST, preferred_element_type=jnp.float32
        )
        pot = jnp.zeros_like(q)
        dz = jnp.zeros_like(q)
        for k in range(8):
            uc = u[8 * k : 8 * k + 8]
            us = u[64 + 8 * k : 72 + 8 * k]
            pot = pot + zrow[0][k] * uc + zrow[1][k] * us
            if k:
                dz = dz + float(k) * (zrow[0][k] * us - zrow[1][k] * uc)
        dx = jnp.zeros_like(q)
        gc = jnp.zeros_like(q)
        gs = jnp.zeros_like(q)
        for k0 in range(8):
            parts = []
            for kind in range(2):
                if k0 == 0 and kind == 1:
                    continue
                j = 2 * k0 + kind
                hc = h[16 * j : 16 * j + 8]
                hs = h[16 * j + 8 : 16 * j + 16]
                parts.append(hc * yc + hs * ys)
                gc = gc + xrow[k0][kind] * hc
                gs = gs + xrow[k0][kind] * hs
            if k0:
                dx = dx + float(k0) * (xrow[k0][0] * parts[1] - xrow[k0][1] * parts[0])
        k1 = iota(q.shape, 0).astype(jnp.float32)
        dy = k1 * (yc * gs - ys * gc)
        edge = -float(TOP) * es * h[16:24]
        total = lambda v: jnp.sum(v, axis=0, keepdims=True)
        fx = total(dx) + edge[0:1] + edge[1:2]
        fy = total(dy) + edge[2:3] + edge[3:4]
        fz = total(dz * q) + edge[4:5] + edge[5:6]
        pot = scale_pot * pot
        forces = [-scale_force * v for v in (fx, fy, fz)]
        for out, cut in ((mine_ref, slice(0, 128)), (send_ref, slice(128, 256))):
            out[chan * frame : chan * frame + chan, :] = pot[:, cut]
            for d in range(3):
                at = half * chan + 3 * frame + d
                out[at : at + 1, :] = forces[d][:, cut]
            at = half * (chan + 3) + frame
            out[at : at + 1, :] = jnp.broadcast_to(energy, (1, 128))


def join_kernel(half, chan, mine_ref, theirs_ref, pot_ref, force_ref, energy_ref):
    side = lax.rem(lax.axis_index("wave"), 2)
    for ref, which in ((mine_ref, side), (theirs_ref, 1 - side)):
        for f in range(half):
            to = which * half + f
            pot_ref[to] = ref[chan * f : chan * f + chan, :]
            for d in range(3):
                at = half * chan + 3 * f + d
                force_ref[d, pl.ds(to, 1), :] = ref[at : at + 1, :]
            energy_ref[to] = ref[half * (chan + 3) + f, 0]


VMEM = pl.BlockSpec(memory_space=pltpu.VMEM)
SMEM = pl.BlockSpec(memory_space=pltpu.SMEM)


def per_device(positions, charges, lattice):
    frames, chan, width = charges.shape
    rows, columns = lax.axis_size("atom"), lax.axis_size("wave")
    atoms = width * rows
    pref = 1.0 / math.sqrt(atoms)
    half = frames // 2
    tiles = width // 128
    assert width // columns == 128 and columns == 4 and rows % 4 == 0
    size = half * tiles * (chan + 3)
    hbm = pl.BlockSpec(memory_space=pltpu.HBM)
    full, own, waves = pl.pallas_call(
        functools.partial(pack_kernel, half, tiles),
        out_shape=(
            jax.ShapeDtypeStruct((2 * size, 128), jnp.float32),
            jax.ShapeDtypeStruct((size, 128), jnp.float32),
            jax.ShapeDtypeStruct((16, 128), jnp.float32),
        ),
        in_specs=[hbm] * 3,
        out_specs=(VMEM, VMEM, VMEM),
        scratch_shapes=[
            pltpu.VMEM((3, frames, width), jnp.float32),
            pltpu.VMEM((frames, chan, width), jnp.bfloat16),
            pltpu.VMEM((3, width), jnp.int32),
            pltpu.SemaphoreType.DMA((3,)),
        ],
        compiler_params=pltpu.CompilerParams(vmem_limit_bytes=4 * 2**20),
    )(
        *(
            pltpu.with_memory_space_constraint(v, pltpu.HBM)
            for v in (positions.transpose(1, 0, 2), charges, lattice)
        )
    )

    def send_to(value, target):
        pairs = []
        for a in range(rows):
            for b in range(columns):
                to, on = target(a, b)
                pairs.append((a * columns + b, to * columns + on))
        return lax.ppermute(value, ("atom", "wave"), pairs)

    first = send_to(full, lambda a, b: (a ^ (1 + b % 2), b))
    second = [send_to(own, lambda a, b, k=k: (a ^ k, b)) for k in range(3, rows)]
    scratch = lambda n: [
        pltpu.VMEM((2, 256, n), jnp.bfloat16),
        pltpu.VMEM((2, 128, n), jnp.bfloat16),
        pltpu.VMEM((2, 32, width), jnp.float32),
    ]

    def partial_sums(blocks, rest=()):
        n = width * (len(blocks) + sum(r.shape[0] for r in rest))
        return pl.pallas_call(
            functools.partial(sums_kernel, half, chan, tiles, len(blocks), len(rest)),
            out_shape=jax.ShapeDtypeStruct((half, 256, 128), jnp.float32),
            in_specs=[VMEM] * (len(blocks) + len(rest)),
            out_specs=VMEM,
            scratch_shapes=scratch(n),
            compiler_params=pltpu.CompilerParams(
                vmem_limit_bytes=(40 if rest else 8) * 2**20
            ),
            cost_estimate=pl.CostEstimate(
                flops=half * 2 * 256 * 128 * n, bytes_accessed=half * 2**18, transcendentals=0
            ),
        )(*blocks, *rest)

    t_own = partial_sums([own])
    across = lax.ppermute(waves, "wave", [(b, b ^ 2) for b in range(columns)])
    first, t_own, across, *second = lax.optimization_barrier((first, t_own, across, *second))
    passed = lax.ppermute(
        jnp.concatenate([first[size:], waves, across], 0),
        "wave",
        [(b, b ^ 1) for b in range(columns)],
    )
    rest = [jnp.stack(second[1:])] if rows > 4 else []
    t_two = partial_sums([first, second[0]], rest)
    result = -(-half * (chan + 4) // 8) * 8
    body = functools.partial(
        kernel,
        half,
        chan,
        tiles,
        2.0 * pref,
        2.0 * TWO_PI * pref / BOX,
        pref / atoms,
    )
    piece = jax.ShapeDtypeStruct((result, 128), jnp.float32)
    mine, send = pl.pallas_call(
        body,
        out_shape=(piece, piece),
        in_specs=[VMEM] * 6,
        out_specs=(VMEM, VMEM),
        scratch_shapes=scratch(width),
        compiler_params=pltpu.CompilerParams(vmem_limit_bytes=8 * 2**20),
    )(own, waves, across, t_own, t_two, passed)
    theirs = lax.ppermute(send, "wave", [(b, b ^ 1) for b in range(columns)])
    pot, force, energy = pl.pallas_call(
        functools.partial(join_kernel, half, chan),
        out_shape=(
            jax.ShapeDtypeStruct((frames, chan, 128), jnp.float32),
            jax.ShapeDtypeStruct((3, frames, 128), jnp.float32),
            jax.ShapeDtypeStruct((frames,), jnp.float32),
        ),
        in_specs=[VMEM, VMEM],
        out_specs=(VMEM, VMEM, SMEM),
        compiler_params=pltpu.CompilerParams(vmem_limit_bytes=4 * 2**20),
    )(mine, theirs)
    return pot, force.transpose(1, 0, 2), energy


def solution(mesh):
    return jax.shard_map(
        per_device,
        mesh=mesh,
        in_specs=(
            P(None, None, ("group", "atom")),
            P(None, None, ("group", "atom")),
            P(None, "wave"),
        ),
        out_specs=(
            P(None, None, ("group", "atom", "wave")),
            P(None, None, ("group", "atom", "wave")),
            P("group"),
        ),
        check_vma=False,
    )
```

```python
import functools
import math

import jax
import jax.numpy as jnp
from jax import lax
from jax.experimental import pallas as pl
from jax.experimental.pallas import tpu as pltpu
from jax.sharding import PartitionSpec as P

BOX = 32
TWO_PI = 2.0 * math.pi
GAUSS = 256.0
TOP = 8

SIN = (3.14159265, -5.16771008, 2.55007753, -0.59829131, 0.07765766)
COS = (1.0, -4.93479283, 4.05841139, -1.33187667, 0.21968962)

NT = (((1,), (1,)), ((), ()))
NN = (((1,), (0,)), ((), ()))
TN = (((0,), (0,)), ((), ()))


def horner(coefs, u):
    value = jnp.full_like(u, coefs[-1])
    for c in coefs[-2::-1]:
        value = value * u + c
    return value


def cos_sin(turns):
    r = turns - jnp.round(turns)
    u = r * r
    s = r * horner(SIN, u)
    c = horner(COS, u)
    return 1.0 - 2.0 * (s * s), 2.0 * (s * c)


def iota(shape, dim):
    return lax.broadcasted_iota(jnp.int32, shape, dim)


def bases(x, y, z):
    k = iota(x.shape, 0)
    kf = k.astype(jnp.float32)
    out = [cos_sin(kf * v) for v in (x, y, z)]
    last = jnp.where(k < 2, x, jnp.where(k < 4, y, z))
    quarter = jnp.where((k & 1) == 1, 0.25, 0.0)
    out.append(cos_sin(TOP * last - quarter))
    return out


def weights(blocks):
    counts = jnp.zeros((64, 32), jnp.float32)
    ends = jnp.zeros((8, 128), jnp.float32)
    for block in blocks:
        n0, n1, n2 = block
        n = n0.shape[1]
        a0, a1, a2 = jnp.abs(n0), jnp.abs(n1), jnp.abs(n2)
        one = jnp.ones_like(n0)
        zero = jnp.zeros_like(n0)

        def sgn(v):
            return jnp.where(v > 0, one, jnp.where(v < 0, -one, zero))

        s0, s1, s2 = sgn(n0), sgn(n1), sgn(n2)
        row = iota((64, n), 0)
        key = ((row // 8) * 16 + row % 8).astype(jnp.float32)
        left = jnp.where(key == a0 * 16.0 + a1, 1.0, 0.0)
        row8 = iota((8, n), 0)
        k8 = row8.astype(jnp.float32)
        hit = k8 == a2
        right = jnp.concatenate(
            [jnp.where(hit, s, 0.0) for s in (one, s1 * s2, s0 * s2, s0 * s1)], 0
        )
        counts += lax.dot_general(
            left.astype(jnp.bfloat16),
            right.astype(jnp.bfloat16),
            NT,
            preferred_element_type=jnp.float32,
        )
        size = jnp.where(row8 < 2, a0, jnp.where(row8 < 4, a1, a2))
        end = jnp.where(size == TOP, 1.0, 0.0)
        for j in range(0, n, 128):
            ends += end[:, j : j + 128]
    row = iota((64, 128), 0)
    lane = iota((64, 128), 1)
    k0, k1, k2 = row // 8, row % 8, (lane // 8) % 8
    square = (k0 * k0 + k1 * k1 + k2 * k2).astype(jnp.float32)
    some = square > 0
    safe = jnp.where(some, square, 1.0)
    gauss = jnp.where(some, jnp.exp(-safe / GAUSS) / safe, 0.0)
    source = iota((32, 128), 0)
    target = iota((32, 128), 1)
    tau = jnp.where(target < 64, 1.0, -1.0)
    out = []
    for v in range(4):
        pick = jnp.where(source == v * 8 + (target // 8) % 8, 1.0, 0.0)
        if v in (1, 2):
            pick = pick * tau
        spread = lax.dot_general(
            counts.astype(jnp.bfloat16),
            pick.astype(jnp.bfloat16),
            NN,
            preferred_element_type=jnp.float32,
        )
        out.append(gauss * spread)
    number = jnp.sum(ends, axis=1, keepdims=True)
    edge = math.exp(-TOP * TOP / GAUSS) / (TOP * TOP)
    keep = (iota((8, 128), 1) < 8) & (iota((8, 128), 0) < 6)
    return out, jnp.where(keep, edge * number, 0.0)


def spectrum(t, w, ends):
    tile = lambda j, y: t[16 * j + 8 * y : 16 * j + 8 * y + 8]
    turn = lambda v: pltpu.roll(v, 64, 1)
    out = []
    for k0 in range(8):
        w0, w1, w2, w3 = (v[8 * k0 : 8 * k0 + 8] for v in w)
        for x in range(2):
            if k0 == 0 and x == 1:
                out.append(ends * tile(1, 0))
                out.append(jnp.zeros_like(ends))
                continue
            for y in range(2):
                sy = 1.0 if y == 0 else -1.0
                sx = 1.0 if x == 0 else -1.0
                m = w0 * tile(2 * k0 + x, y) - sy * w1 * turn(tile(2 * k0 + x, 1 - y))
                if k0:
                    m = m - sx * w2 * turn(tile(2 * k0 + 1 - x, y))
                    m = m - sx * sy * w3 * tile(2 * k0 + 1 - x, 1 - y)
                out.append(m)
    return jnp.concatenate(out, 0)


def lines(block, first, tiles):
    return jnp.concatenate([block[first + t : first + t + 1] for t in range(tiles)], 1)


def tall(line):
    return jnp.broadcast_to(line, (8, line.shape[1]))


def pack_kernel(
    half, tiles, pos_hbm, charge_hbm, lattice_hbm, full_ref, own_ref, near_ref, pos_ref, charge_ref, lattice_ref, sem
):
    copies = [
        pltpu.make_async_copy(a, b, sem.at[i])
        for i, (a, b) in enumerate(
            ((charge_hbm, charge_ref), (pos_hbm, pos_ref), (lattice_hbm, lattice_ref))
        )
    ]
    for c in copies:
        c.start()
    for c in copies:
        c.wait()
    mine = lax.rem(lax.axis_index("wave"), 2)
    chan = charge_ref.shape[1]
    cut = lambda t: slice(128 * t, 128 * t + 128)
    row = 0
    for side, outs in ((mine, (full_ref, own_ref)), (1 - mine, (full_ref,))):
        for f in range(half):
            q = charge_ref[side * half + f].astype(jnp.float32)
            for t in range(tiles):
                for out in outs:
                    out[row : row + chan, :] = q[:, cut(t)]
                row += chan
        for f in range(half):
            for d in range(3):
                line = pos_ref[d, pl.ds(side * half + f, 1), :]
                for t in range(tiles):
                    for out in outs:
                        out[row : row + 1, :] = line[:, cut(t)]
                    row += 1
    own_ref[row // 2 :, :] = jnp.zeros((own_ref.shape[0] - row // 2, 128), jnp.float32)
    lattice = lattice_ref[...].astype(jnp.float32)
    for d in range(3):
        for t in range(tiles):
            row = d * tiles + t
            near_ref[row : row + 1, :] = lattice[d : d + 1, cut(t)]


def spread(ref, row):
    return tall(ref[pl.ds(row, 1), :])


def place(block, frame, first, picks):
    return [
        jnp.concatenate(
            [spread(block, first + (frame * 3 + d) * picks[0] + t) for t in picks[1]], 1
        )
        for d in range(3)
    ]


def fill(block, chan, tiles, half, frame, a_ref, b_ref, table, base):
    x, y, z = place(block, frame, half * tiles * chan, (tiles, range(tiles)))
    (xc, xs), (yc, ys), (zc, zs), (ec, _) = bases(x, y, z)
    q = jnp.concatenate(
        [block[pl.ds((frame * tiles + t) * chan, chan), :] for t in range(tiles)], 1
    )
    table[0:8] = xc
    table[8:16] = xs
    table[16:24] = zc
    table[24:32] = zs
    columns = pl.ds(base, 128 * tiles)
    for k0 in range(8):
        for kind in range(2):
            j = 2 * k0 + kind
            if j == 1:
                value = jnp.concatenate([ec, ec], 0)
            else:
                f = spread(table, 8 * kind + k0)
                value = jnp.concatenate([f * yc, f * ys], 0)
            a_ref[16 * j : 16 * j + 16, columns] = value.astype(jnp.bfloat16)
    for kind in range(2):
        for k in range(0, 8, 2):
            j = 8 * kind + k
            value = jnp.concatenate([spread(table, 16 + j) * q, spread(table, 17 + j) * q], 0)
            b_ref[8 * j : 8 * j + 16, columns] = value.astype(jnp.bfloat16)


def sums(blocks, rest, half, chan, tiles, frame, a_ref, b_ref, basis):
    width = 128 * tiles
    a, b = a_ref.at[frame % 2], b_ref.at[frame % 2]
    for slot, block in enumerate(blocks):
        fill(block, chan, tiles, half, frame, a, b, basis.at[slot % 2], slot * width)
    for ref in rest:

        @pl.loop(0, ref.shape[0])
        def _(i):
            base = pl.multiple_of((i + len(blocks)) * width, width)
            fill(ref.at[i], chan, tiles, half, frame, a, b, basis.at[0], base)

    return lax.dot_general(a[...], b[...], NT, preferred_element_type=jnp.float32)


def sums_kernel(half, chan, tiles, count, more, *refs):
    blocks, rest = refs[:count], refs[count : count + more]
    t_ref, a_ref, b_ref, basis = refs[count + more :]
    for frame in range(half):
        t_ref[frame] = sums(blocks, rest, half, chan, tiles, frame, a_ref, b_ref, basis)


def split(value):
    high = value.astype(jnp.bfloat16)
    return high, (value - high.astype(jnp.float32)).astype(jnp.bfloat16)


def early_kernel(half, chan, tiles, own, t_ref, line_ref, atom_ref, load_ref, a_ref, b_ref, basis):
    here = lax.axis_index("wave")
    pair = (here, here + 1 - 2 * lax.rem(here, 2))
    for frame in range(half):
        t_ref[frame] = sums((own,), (), half, chan, tiles, frame, a_ref, b_ref, basis)
        x, y, z = place(own, frame, half * tiles * chan, (tiles, pair))
        (xc, xs), (yc, ys), (zc, zs), (ec, es) = bases(x, y, z)
        q = jnp.concatenate(
            [
                own[pl.ds(pl.multiple_of((frame * tiles + p) * chan, chan), chan), :]
                for p in pair
            ],
            1,
        )
        line_ref[frame] = jnp.concatenate([xc, xs, yc, ys, zc, zs, es, q], 0)
        for k0 in range(8):
            for kind, x in enumerate((xc, xs)):
                f = tall(x[k0 : k0 + 1])
                if k0 == 0 and kind == 1:
                    value = jnp.concatenate([ec, jnp.zeros_like(ec)], 0)
                else:
                    value = jnp.concatenate([f * yc, f * ys], 0)
                at = 16 * (2 * k0 + kind)
                high, low = split(value)
                atom_ref[frame, 0, at : at + 16] = high
                atom_ref[frame, 1, at : at + 16] = low
        for kind, z in enumerate((zc, zs)):
            for k in range(0, 8, 2):
                value = jnp.concatenate([tall(z[k : k + 1]) * q, tall(z[k + 1 : k + 2]) * q], 0)
                at = 8 * (8 * kind + k)
                high, low = split(value)
                load_ref[frame, at : at + 16] = high
                load_ref[frame, 128 + at : 144 + at] = high
                load_ref[frame, 256 + at : 272 + at] = low


def kernel(half, chan, tiles, scale_pot, scale_force, scale_energy, *refs):
    t_ref, u_ref, line_ref, atom_ref, load_ref = refs[:5]
    pass_ref, last_ref, near, beside, across = refs[5:10]
    mine_ref, send_ref, a_ref, b_ref, basis = refs[10:]
    blocks = []
    for ref, at in ((near, 0), (beside, 0), (across, 0), (across, 16)):
        v = ref[at : at + 3 * tiles, :]
        blocks.append([lines(v, d * tiles, tiles) for d in range(3)])
    w, ends = weights(blocks)
    dot = functools.partial(lax.dot_general, preferred_element_type=jnp.float32)
    ts = [
        t_ref[frame]
        + u_ref[frame]
        + sums((pass_ref, last_ref), (), half, chan, tiles, frame, a_ref, b_ref, basis)
        for frame in range(half)
    ]
    ms = [spectrum(t, w, ends) for t in ts]
    backs, outs = [], []
    for frame in range(half):
        high, low = split(ms[frame])
        backs.append(
            dot(jnp.concatenate([high, low], 1), load_ref[frame, 0:256], NN)
            + dot(high, load_ref[frame, 256:384], NN)
        )
        outs.append(
            dot(high, atom_ref[frame, 0], TN)
            + dot(high, atom_ref[frame, 1], TN)
            + dot(low, atom_ref[frame, 0], TN)
        )
    for frame in range(half):
        energy = scale_energy * jnp.sum(
            jnp.sum(ts[frame] * ms[frame], 0, keepdims=True), 1, keepdims=True
        )
        h, u = backs[frame], outs[frame]
        xc, xs, yc, ys, zc, zs, es, q = (line_ref[frame, 8 * i : 8 * i + 8] for i in range(8))
        row = lambda v, k: jnp.broadcast_to(v[k : k + 1], v.shape)
        xrow = [(row(xc, k), row(xs, k)) for k in range(8)]
        zrow = [[row(v, k) for k in range(8)] for v in (zc, zs)]
        pot = jnp.zeros_like(q)
        dz = jnp.zeros_like(q)
        for k in range(8):
            uc = u[8 * k : 8 * k + 8]
            us = u[64 + 8 * k : 72 + 8 * k]
            pot = pot + zrow[0][k] * uc + zrow[1][k] * us
            if k:
                dz = dz + float(k) * (zrow[0][k] * us - zrow[1][k] * uc)
        dx = jnp.zeros_like(q)
        gc = jnp.zeros_like(q)
        gs = jnp.zeros_like(q)
        for k0 in range(8):
            parts = []
            for kind in range(2):
                if k0 == 0 and kind == 1:
                    continue
                j = 2 * k0 + kind
                hc = h[16 * j : 16 * j + 8]
                hs = h[16 * j + 8 : 16 * j + 16]
                parts.append(hc * yc + hs * ys)
                gc = gc + xrow[k0][kind] * hc
                gs = gs + xrow[k0][kind] * hs
            if k0:
                dx = dx + float(k0) * (xrow[k0][0] * parts[1] - xrow[k0][1] * parts[0])
        k1 = iota(q.shape, 0).astype(jnp.float32)
        dy = k1 * (yc * gs - ys * gc)
        edge = -float(TOP) * es * h[16:24]
        total = lambda v: jnp.sum(v, axis=0, keepdims=True)
        fx = total(dx) + edge[0:1] + edge[1:2]
        fy = total(dy) + edge[2:3] + edge[3:4]
        fz = total(dz * q) + edge[4:5] + edge[5:6]
        pot = scale_pot * pot
        forces = [-scale_force * v for v in (fx, fy, fz)]
        for out, cut in ((mine_ref, slice(0, 128)), (send_ref, slice(128, 256))):
            out[chan * frame : chan * frame + chan, :] = pot[:, cut]
            for d in range(3):
                at = half * chan + 3 * frame + d
                out[at : at + 1, :] = forces[d][:, cut]
            at = half * (chan + 3) + frame
            out[at : at + 1, :] = jnp.broadcast_to(energy, (1, 128))


def join_kernel(half, chan, mine_ref, theirs_ref, pot_ref, force_ref, energy_ref):
    side = lax.rem(lax.axis_index("wave"), 2)
    for ref, which in ((mine_ref, side), (theirs_ref, 1 - side)):
        for f in range(half):
            to = which * half + f
            pot_ref[to] = ref[chan * f : chan * f + chan, :]
            for d in range(3):
                at = half * chan + 3 * f + d
                force_ref[d, pl.ds(to, 1), :] = ref[at : at + 1, :]
            energy_ref[to] = ref[half * (chan + 3) + f, 0]


COST = 1
PAD = 64
VMEM = pl.BlockSpec(memory_space=pltpu.VMEM)
SMEM = pl.BlockSpec(memory_space=pltpu.SMEM)


def per_device(positions, charges, lattice):
    frames, chan, width = charges.shape
    rows, columns = lax.axis_size("atom"), lax.axis_size("wave")
    atoms = width * rows
    pref = 1.0 / math.sqrt(atoms)
    half = frames // 2
    tiles = width // 128
    assert width // columns == 128 and columns == 4 and rows % 4 == 0
    size = half * tiles * (chan + 3)
    hbm = pl.BlockSpec(memory_space=pltpu.HBM)
    full, own, near = pl.pallas_call(
        functools.partial(pack_kernel, half, tiles),
        out_shape=(
            jax.ShapeDtypeStruct((2 * size, 128), jnp.float32),
            jax.ShapeDtypeStruct((size + 16, 128), jnp.float32),
            jax.ShapeDtypeStruct((16, 128), jnp.float32),
        ),
        in_specs=[hbm] * 3,
        out_specs=(VMEM, VMEM, VMEM),
        scratch_shapes=[
            pltpu.VMEM((3, frames, width), jnp.float32),
            pltpu.VMEM((frames, chan, width), jnp.bfloat16),
            pltpu.VMEM((3, width), jnp.int32),
            pltpu.SemaphoreType.DMA((3,)),
        ],
        compiler_params=pltpu.CompilerParams(vmem_limit_bytes=4 * 2**20),
    )(
        *(
            pltpu.with_memory_space_constraint(v, pltpu.HBM)
            for v in (positions.transpose(1, 0, 2), charges, lattice)
        )
    )

    def send_to(value, target):
        pairs = []
        for a in range(rows):
            for b in range(columns):
                to, on = target(a, b)
                pairs.append((a * columns + b, to * columns + on))
        return lax.ppermute(value, ("atom", "wave"), pairs)

    first = send_to(full, lambda a, b: (a ^ (1 + b % 2), b))
    second = [send_to(own, lambda a, b, k=k: (a ^ k, b)) for k in range(3, rows)]
    scratch = lambda n: [
        pltpu.VMEM((2, 256, n), jnp.bfloat16),
        pltpu.VMEM((2, 128, n), jnp.bfloat16),
        pltpu.VMEM((2, 32, width), jnp.float32),
    ]

    f32 = lambda *shape: jax.ShapeDtypeStruct(shape, jnp.float32)
    bf16 = lambda *shape: jax.ShapeDtypeStruct(shape, jnp.bfloat16)

    def call(body, blocks, out_shape, args, limit=8):
        return pl.pallas_call(
            body,
            out_shape=out_shape,
            in_specs=[VMEM] * len(args),
            out_specs=tuple(VMEM for _ in out_shape),
            scratch_shapes=scratch(width * blocks),
            compiler_params=pltpu.CompilerParams(vmem_limit_bytes=limit * 2**20),
            cost_estimate=pl.CostEstimate(
                flops=COST, bytes_accessed=COST, transcendentals=0
            ),
        )(*args)

    totals = f32(half, 256, 128)
    t_own, line, atom, load = call(
        functools.partial(early_kernel, half, chan, tiles),
        1,
        (totals, f32(half, 64, 256), bf16(half, 2, 256, 256), bf16(half, 384, 256)),
        (own,),
    )
    beside = lax.ppermute(near, "wave", [(b, b ^ 1) for b in range(columns)])
    both = jnp.concatenate([near, beside, jnp.zeros((PAD, 128), jnp.float32)], 0)
    across = lax.ppermute(both, "wave", [(b, b ^ 2) for b in range(columns)])
    first, t_own = lax.optimization_barrier((first, t_own))
    passed = lax.ppermute(first[size:], "wave", [(b, b ^ 1) for b in range(columns)])
    (t_two,) = call(
        functools.partial(sums_kernel, half, chan, tiles, 1, 0), 1, (totals,), (first,)
    )
    if rows > 4:
        (t_rest,) = call(
            functools.partial(sums_kernel, half, chan, tiles, 0, 1),
            rows - 4,
            (totals,),
            (jnp.stack(second[1:]),),
            40,
        )
        t_two = t_two + t_rest
    result = -(-half * (chan + 4) // 8) * 8
    mine, send = call(
        functools.partial(
            kernel,
            half,
            chan,
            tiles,
            2.0 * pref,
            2.0 * TWO_PI * pref / BOX,
            pref / atoms,
        ),
        2,
        (f32(result, 128), f32(result, 128)),
        (t_own, t_two, line, atom, load, passed, second[0], near, beside, across),
    )
    theirs = lax.ppermute(send, "wave", [(b, b ^ 1) for b in range(columns)])
    pot, force, energy = pl.pallas_call(
        functools.partial(join_kernel, half, chan),
        out_shape=(
            jax.ShapeDtypeStruct((frames, chan, 128), jnp.float32),
            jax.ShapeDtypeStruct((3, frames, 128), jnp.float32),
            jax.ShapeDtypeStruct((frames,), jnp.float32),
        ),
        in_specs=[VMEM, VMEM],
        out_specs=(VMEM, VMEM, SMEM),
        compiler_params=pltpu.CompilerParams(vmem_limit_bytes=4 * 2**20),
    )(mine, theirs)
    return pot, force.transpose(1, 0, 2), energy


def solution(mesh):
    return jax.shard_map(
        per_device,
        mesh=mesh,
        in_specs=(
            P(None, None, ("group", "atom")),
            P(None, None, ("group", "atom")),
            P(None, "wave"),
        ),
        out_specs=(
            P(None, None, ("group", "atom", "wave")),
            P(None, None, ("group", "atom", "wave")),
            P("group"),
        ),
        check_vma=False,
    )
```

```python
import functools
import math

import jax
import jax.numpy as jnp
from jax import lax
from jax.experimental import pallas as pl
from jax.experimental.pallas import tpu as pltpu
from jax.sharding import PartitionSpec as P

BOX = 32
TWO_PI = 2.0 * math.pi
GAUSS = 256.0
TOP = 8

SIN = (3.14159265, -5.16771008, 2.55007753, -0.59829131, 0.07765766)
COS = (1.0, -4.93479283, 4.05841139, -1.33187667, 0.21968962)

NT = (((1,), (1,)), ((), ()))
NN = (((1,), (0,)), ((), ()))
TN = (((0,), (0,)), ((), ()))


def horner(coefs, u):
    value = jnp.full_like(u, coefs[-1])
    for c in coefs[-2::-1]:
        value = value * u + c
    return value


def cos_sin(turns):
    r = turns - jnp.round(turns)
    u = r * r
    s = r * horner(SIN, u)
    c = horner(COS, u)
    return 1.0 - 2.0 * (s * s), 2.0 * (s * c)


def iota(shape, dim):
    return lax.broadcasted_iota(jnp.int32, shape, dim)


def bases(x, y, z):
    k = iota(x.shape, 0)
    kf = k.astype(jnp.float32)
    out = [cos_sin(kf * v) for v in (x, y, z)]
    last = jnp.where(k < 2, x, jnp.where(k < 4, y, z))
    quarter = jnp.where((k & 1) == 1, 0.25, 0.0)
    out.append(cos_sin(TOP * last - quarter))
    return out


def census(blocks, counts, ends):
    for block in blocks:
        n0, n1, n2 = block
        n = n0.shape[1]
        a0, a1, a2 = jnp.abs(n0), jnp.abs(n1), jnp.abs(n2)
        one = jnp.ones_like(n0)
        zero = jnp.zeros_like(n0)

        def sgn(v):
            return jnp.where(v > 0, one, jnp.where(v < 0, -one, zero))

        s0, s1, s2 = sgn(n0), sgn(n1), sgn(n2)
        row = iota((64, n), 0)
        key = ((row // 8) * 16 + row % 8).astype(jnp.float32)
        left = jnp.where(key == a0 * 16.0 + a1, 1.0, 0.0)
        row8 = iota((8, n), 0)
        k8 = row8.astype(jnp.float32)
        hit = k8 == a2
        right = jnp.concatenate(
            [jnp.where(hit, s, 0.0) for s in (one, s1 * s2, s0 * s2, s0 * s1)], 0
        )
        counts += lax.dot_general(
            left.astype(jnp.bfloat16),
            right.astype(jnp.bfloat16),
            NT,
            preferred_element_type=jnp.float32,
        )
        size = jnp.where(row8 < 2, a0, jnp.where(row8 < 4, a1, a2))
        end = jnp.where(size == TOP, 1.0, 0.0)
        for j in range(0, n, 128):
            ends += end[:, j : j + 128]
    return counts, ends


def weights(counts, ends):
    row = iota((64, 128), 0)
    lane = iota((64, 128), 1)
    k0, k1, k2 = row // 8, row % 8, (lane // 8) % 8
    square = (k0 * k0 + k1 * k1 + k2 * k2).astype(jnp.float32)
    some = square > 0
    safe = jnp.where(some, square, 1.0)
    gauss = jnp.where(some, jnp.exp(-safe / GAUSS) / safe, 0.0)
    source = iota((32, 128), 0)
    target = iota((32, 128), 1)
    tau = jnp.where(target < 64, 1.0, -1.0)
    out = []
    for v in range(4):
        pick = jnp.where(source == v * 8 + (target // 8) % 8, 1.0, 0.0)
        if v in (1, 2):
            pick = pick * tau
        spread = lax.dot_general(
            counts.astype(jnp.bfloat16),
            pick.astype(jnp.bfloat16),
            NN,
            preferred_element_type=jnp.float32,
        )
        out.append(gauss * spread)
    number = jnp.sum(ends, axis=1, keepdims=True)
    edge = math.exp(-TOP * TOP / GAUSS) / (TOP * TOP)
    keep = (iota((8, 128), 1) < 8) & (iota((8, 128), 0) < 6)
    return out, jnp.where(keep, edge * number, 0.0)


def spectrum(t, w, ends):
    tile = lambda j, y: t[16 * j + 8 * y : 16 * j + 8 * y + 8]
    turn = lambda v: pltpu.roll(v, 64, 1)
    out = []
    for k0 in range(8):
        w0, w1, w2, w3 = (v[8 * k0 : 8 * k0 + 8] for v in w)
        for x in range(2):
            if k0 == 0 and x == 1:
                out.append(ends * tile(1, 0))
                out.append(jnp.zeros_like(ends))
                continue
            for y in range(2):
                sy = 1.0 if y == 0 else -1.0
                sx = 1.0 if x == 0 else -1.0
                m = w0 * tile(2 * k0 + x, y) - sy * w1 * turn(tile(2 * k0 + x, 1 - y))
                if k0:
                    m = m - sx * w2 * turn(tile(2 * k0 + 1 - x, y))
                    m = m - sx * sy * w3 * tile(2 * k0 + 1 - x, 1 - y)
                out.append(m)
    return jnp.concatenate(out, 0)


def lines(block, first, tiles):
    return jnp.concatenate([block[first + t : first + t + 1] for t in range(tiles)], 1)


def tall(line):
    return jnp.broadcast_to(line, (8, line.shape[1]))


def pack_kernel(
    half, tiles, pos_hbm, charge_hbm, lattice_hbm, full_ref, own_ref, near_ref, pos_ref, charge_ref, lattice_ref, sem
):
    copies = [
        pltpu.make_async_copy(a, b, sem.at[i])
        for i, (a, b) in enumerate(
            ((charge_hbm, charge_ref), (pos_hbm, pos_ref), (lattice_hbm, lattice_ref))
        )
    ]
    for c in copies:
        c.start()
    for c in copies:
        c.wait()
    mine = lax.rem(lax.axis_index("wave"), 2)
    chan = charge_ref.shape[1]
    cut = lambda t: slice(128 * t, 128 * t + 128)
    row = 0
    for side, outs in ((mine, (full_ref, own_ref)), (1 - mine, (full_ref,))):
        for f in range(half):
            q = charge_ref[side * half + f].astype(jnp.float32)
            for t in range(tiles):
                for out in outs:
                    out[row : row + chan, :] = q[:, cut(t)]
                row += chan
        for f in range(half):
            for d in range(3):
                line = pos_ref[d, pl.ds(side * half + f, 1), :]
                for t in range(tiles):
                    for out in outs:
                        out[row : row + 1, :] = line[:, cut(t)]
                    row += 1
    own_ref[row // 2 :, :] = jnp.zeros((own_ref.shape[0] - row // 2, 128), jnp.float32)
    lattice = lattice_ref[...].astype(jnp.float32)
    for d in range(3):
        for t in range(tiles):
            row = d * tiles + t
            near_ref[row : row + 1, :] = lattice[d : d + 1, cut(t)]


def spread(ref, row):
    return tall(ref[pl.ds(row, 1), :])


def place(block, frame, first, picks):
    return [
        jnp.concatenate(
            [spread(block, first + (frame * 3 + d) * picks[0] + t) for t in picks[1]], 1
        )
        for d in range(3)
    ]


def fill(block, chan, tiles, half, frame, a_ref, b_ref, table, base):
    x, y, z = place(block, frame, half * tiles * chan, (tiles, range(tiles)))
    (xc, xs), (yc, ys), (zc, zs), (ec, _) = bases(x, y, z)
    q = jnp.concatenate(
        [block[pl.ds((frame * tiles + t) * chan, chan), :] for t in range(tiles)], 1
    )
    table[0:8] = xc
    table[8:16] = xs
    table[16:24] = zc
    table[24:32] = zs
    columns = pl.ds(base, 128 * tiles)
    for k0 in range(8):
        for kind in range(2):
            j = 2 * k0 + kind
            if j == 1:
                value = jnp.concatenate([ec, ec], 0)
            else:
                f = spread(table, 8 * kind + k0)
                value = jnp.concatenate([f * yc, f * ys], 0)
            a_ref[16 * j : 16 * j + 16, columns] = value.astype(jnp.bfloat16)
    for kind in range(2):
        for k in range(0, 8, 2):
            j = 8 * kind + k
            value = jnp.concatenate([spread(table, 16 + j) * q, spread(table, 17 + j) * q], 0)
            b_ref[8 * j : 8 * j + 16, columns] = value.astype(jnp.bfloat16)


def sums(blocks, rest, half, chan, tiles, frame, a_ref, b_ref, basis):
    width = 128 * tiles
    a, b = a_ref.at[frame % 2], b_ref.at[frame % 2]
    for slot, block in enumerate(blocks):
        fill(block, chan, tiles, half, frame, a, b, basis.at[slot % 2], slot * width)
    for ref in rest:

        @pl.loop(0, ref.shape[0])
        def _(i):
            base = pl.multiple_of((i + len(blocks)) * width, width)
            fill(ref.at[i], chan, tiles, half, frame, a, b, basis.at[0], base)

    return lax.dot_general(a[...], b[...], NT, preferred_element_type=jnp.float32)


def lattice_blocks(tiles, places):
    blocks = []
    for ref, at in places:
        v = ref[at : at + 3 * tiles, :]
        blocks.append([lines(v, d * tiles, tiles) for d in range(3)])
    return blocks


def pass_kernel(half, chan, tiles, *refs):
    u_ref, pass_ref, near, beside, t_ref, count_ref, end_ref, a_ref, b_ref, basis = refs
    zeros = jnp.zeros((64, 32), jnp.float32), jnp.zeros((8, 128), jnp.float32)
    blocks = lattice_blocks(tiles, ((near, 0), (beside, 0)))
    count_ref[...], end_ref[...] = census(blocks, *zeros)
    for frame in range(half):
        t_ref[frame] = u_ref[frame] + sums(
            (pass_ref,), (), half, chan, tiles, frame, a_ref, b_ref, basis
        )


def sums_kernel(half, chan, tiles, count, more, *refs):
    blocks, rest = refs[:count], refs[count : count + more]
    t_ref, a_ref, b_ref, basis = refs[count + more :]
    for frame in range(half):
        t_ref[frame] = sums(blocks, rest, half, chan, tiles, frame, a_ref, b_ref, basis)


def split(value):
    high = value.astype(jnp.bfloat16)
    return high, (value - high.astype(jnp.float32)).astype(jnp.bfloat16)


def early_kernel(half, chan, tiles, own, t_ref, line_ref, atom_ref, load_ref, a_ref, b_ref, basis):
    here = lax.axis_index("wave")
    pair = (here, here + 1 - 2 * lax.rem(here, 2))
    for frame in range(half):
        t_ref[frame] = sums((own,), (), half, chan, tiles, frame, a_ref, b_ref, basis)
        x, y, z = place(own, frame, half * tiles * chan, (tiles, pair))
        (xc, xs), (yc, ys), (zc, zs), (ec, es) = bases(x, y, z)
        q = jnp.concatenate(
            [
                own[pl.ds(pl.multiple_of((frame * tiles + p) * chan, chan), chan), :]
                for p in pair
            ],
            1,
        )
        line_ref[frame] = jnp.concatenate([xc, xs, yc, ys, zc, zs, es, q], 0)
        for k0 in range(8):
            for kind, x in enumerate((xc, xs)):
                f = tall(x[k0 : k0 + 1])
                if k0 == 0 and kind == 1:
                    value = jnp.concatenate([ec, jnp.zeros_like(ec)], 0)
                else:
                    value = jnp.concatenate([f * yc, f * ys], 0)
                at = 16 * (2 * k0 + kind)
                high, low = split(value)
                atom_ref[frame, 0, at : at + 16] = high
                atom_ref[frame, 1, at : at + 16] = low
        for kind, z in enumerate((zc, zs)):
            for k in range(0, 8, 2):
                value = jnp.concatenate([tall(z[k : k + 1]) * q, tall(z[k + 1 : k + 2]) * q], 0)
                at = 8 * (8 * kind + k)
                high, low = split(value)
                load_ref[frame, at : at + 16] = high
                load_ref[frame, 128 + at : 144 + at] = high
                load_ref[frame, 256 + at : 272 + at] = low


def kernel(half, chan, tiles, scale_pot, scale_force, scale_energy, *refs):
    t_ref, u_ref, line_ref, atom_ref, load_ref = refs[:5]
    count_ref, end_ref, last_ref, across = refs[5:9]
    mine_ref, send_ref, a_ref, b_ref, basis = refs[9:]
    blocks = lattice_blocks(tiles, ((across, 0), (across, 16)))
    w, ends = weights(*census(blocks, count_ref[...], end_ref[...]))
    dot = functools.partial(lax.dot_general, preferred_element_type=jnp.float32)
    ts = [
        t_ref[frame]
        + u_ref[frame]
        + sums((last_ref,), (), half, chan, tiles, frame, a_ref, b_ref, basis)
        for frame in range(half)
    ]
    ms = [spectrum(t, w, ends) for t in ts]
    backs, outs = [], []
    for frame in range(half):
        high, low = split(ms[frame])
        backs.append(
            dot(jnp.concatenate([high, low], 1), load_ref[frame, 0:256], NN)
            + dot(high, load_ref[frame, 256:384], NN)
        )
        outs.append(
            dot(high, atom_ref[frame, 0], TN)
            + dot(high, atom_ref[frame, 1], TN)
            + dot(low, atom_ref[frame, 0], TN)
        )
    for frame in range(half):
        energy = scale_energy * jnp.sum(
            jnp.sum(ts[frame] * ms[frame], 0, keepdims=True), 1, keepdims=True
        )
        h, u = backs[frame], outs[frame]
        xc, xs, yc, ys, zc, zs, es, q = (line_ref[frame, 8 * i : 8 * i + 8] for i in range(8))
        row = lambda v, k: jnp.broadcast_to(v[k : k + 1], v.shape)
        xrow = [(row(xc, k), row(xs, k)) for k in range(8)]
        zrow = [[row(v, k) for k in range(8)] for v in (zc, zs)]
        pot = jnp.zeros_like(q)
        dz = jnp.zeros_like(q)
        for k in range(8):
            uc = u[8 * k : 8 * k + 8]
            us = u[64 + 8 * k : 72 + 8 * k]
            pot = pot + zrow[0][k] * uc + zrow[1][k] * us
            if k:
                dz = dz + float(k) * (zrow[0][k] * us - zrow[1][k] * uc)
        dx = jnp.zeros_like(q)
        gc = jnp.zeros_like(q)
        gs = jnp.zeros_like(q)
        for k0 in range(8):
            parts = []
            for kind in range(2):
                if k0 == 0 and kind == 1:
                    continue
                j = 2 * k0 + kind
                hc = h[16 * j : 16 * j + 8]
                hs = h[16 * j + 8 : 16 * j + 16]
                parts.append(hc * yc + hs * ys)
                gc = gc + xrow[k0][kind] * hc
                gs = gs + xrow[k0][kind] * hs
            if k0:
                dx = dx + float(k0) * (xrow[k0][0] * parts[1] - xrow[k0][1] * parts[0])
        k1 = iota(q.shape, 0).astype(jnp.float32)
        dy = k1 * (yc * gs - ys * gc)
        edge = -float(TOP) * es * h[16:24]
        total = lambda v: jnp.sum(v, axis=0, keepdims=True)
        fx = total(dx) + edge[0:1] + edge[1:2]
        fy = total(dy) + edge[2:3] + edge[3:4]
        fz = total(dz * q) + edge[4:5] + edge[5:6]
        pot = scale_pot * pot
        forces = [-scale_force * v for v in (fx, fy, fz)]
        for out, cut in ((mine_ref, slice(0, 128)), (send_ref, slice(128, 256))):
            out[chan * frame : chan * frame + chan, :] = pot[:, cut]
            for d in range(3):
                at = half * chan + 3 * frame + d
                out[at : at + 1, :] = forces[d][:, cut]
            at = half * (chan + 3) + frame
            out[at : at + 1, :] = jnp.broadcast_to(energy, (1, 128))


def join_kernel(half, chan, mine_ref, theirs_ref, pot_ref, force_ref, energy_ref):
    side = lax.rem(lax.axis_index("wave"), 2)
    for ref, which in ((mine_ref, side), (theirs_ref, 1 - side)):
        for f in range(half):
            to = which * half + f
            pot_ref[to] = ref[chan * f : chan * f + chan, :]
            for d in range(3):
                at = half * chan + 3 * f + d
                force_ref[d, pl.ds(to, 1), :] = ref[at : at + 1, :]
            energy_ref[to] = ref[half * (chan + 3) + f, 0]


COST = 1
PAD = 64
VMEM = pl.BlockSpec(memory_space=pltpu.VMEM)
SMEM = pl.BlockSpec(memory_space=pltpu.SMEM)


def per_device(positions, charges, lattice):
    frames, chan, width = charges.shape
    rows, columns = lax.axis_size("atom"), lax.axis_size("wave")
    atoms = width * rows
    pref = 1.0 / math.sqrt(atoms)
    half = frames // 2
    tiles = width // 128
    assert width // columns == 128 and columns == 4 and rows % 4 == 0
    size = half * tiles * (chan + 3)
    hbm = pl.BlockSpec(memory_space=pltpu.HBM)
    full, own, near = pl.pallas_call(
        functools.partial(pack_kernel, half, tiles),
        out_shape=(
            jax.ShapeDtypeStruct((2 * size, 128), jnp.float32),
            jax.ShapeDtypeStruct((size + 16, 128), jnp.float32),
            jax.ShapeDtypeStruct((16, 128), jnp.float32),
        ),
        in_specs=[hbm] * 3,
        out_specs=(VMEM, VMEM, VMEM),
        scratch_shapes=[
            pltpu.VMEM((3, frames, width), jnp.float32),
            pltpu.VMEM((frames, chan, width), jnp.bfloat16),
            pltpu.VMEM((3, width), jnp.int32),
            pltpu.SemaphoreType.DMA((3,)),
        ],
        compiler_params=pltpu.CompilerParams(vmem_limit_bytes=4 * 2**20),
    )(
        *(
            pltpu.with_memory_space_constraint(v, pltpu.HBM)
            for v in (positions.transpose(1, 0, 2), charges, lattice)
        )
    )

    def send_to(value, target):
        pairs = []
        for a in range(rows):
            for b in range(columns):
                to, on = target(a, b)
                pairs.append((a * columns + b, to * columns + on))
        return lax.ppermute(value, ("atom", "wave"), pairs)

    first = send_to(full, lambda a, b: (a ^ (1 + b % 2), b))
    second = [send_to(own, lambda a, b, k=k: (a ^ k, b)) for k in range(3, rows)]
    scratch = lambda n: [
        pltpu.VMEM((2, 256, n), jnp.bfloat16),
        pltpu.VMEM((2, 128, n), jnp.bfloat16),
        pltpu.VMEM((2, 32, width), jnp.float32),
    ]

    f32 = lambda *shape: jax.ShapeDtypeStruct(shape, jnp.float32)
    bf16 = lambda *shape: jax.ShapeDtypeStruct(shape, jnp.bfloat16)

    def call(body, blocks, out_shape, args, limit=8):
        return pl.pallas_call(
            body,
            out_shape=out_shape,
            in_specs=[VMEM] * len(args),
            out_specs=tuple(VMEM for _ in out_shape),
            scratch_shapes=scratch(width * blocks),
            compiler_params=pltpu.CompilerParams(vmem_limit_bytes=limit * 2**20),
            cost_estimate=pl.CostEstimate(
                flops=COST, bytes_accessed=COST, transcendentals=0
            ),
        )(*args)

    totals = f32(half, 256, 128)
    t_own, line, atom, load = call(
        functools.partial(early_kernel, half, chan, tiles),
        1,
        (totals, f32(half, 64, 256), bf16(half, 2, 256, 256), bf16(half, 384, 256)),
        (own,),
    )
    beside = lax.ppermute(near, "wave", [(b, b ^ 1) for b in range(columns)])
    both = jnp.concatenate([near, beside, jnp.zeros((PAD, 128), jnp.float32)], 0)
    across = lax.ppermute(both, "wave", [(b, b ^ 2) for b in range(columns)])
    first, t_own = lax.optimization_barrier((first, t_own))
    passed = lax.ppermute(first[size:], "wave", [(b, b ^ 1) for b in range(columns)])
    (t_two,) = call(
        functools.partial(sums_kernel, half, chan, tiles, 1, 0), 1, (totals,), (first,)
    )
    t_two, counts, ends = call(
        functools.partial(pass_kernel, half, chan, tiles),
        1,
        (totals, f32(64, 32), f32(8, 128)),
        (t_two, passed, near, beside),
    )
    if rows > 4:
        (t_rest,) = call(
            functools.partial(sums_kernel, half, chan, tiles, 0, 1),
            rows - 4,
            (totals,),
            (jnp.stack(second[1:]),),
            40,
        )
        t_two = t_two + t_rest
    result = -(-half * (chan + 4) // 8) * 8
    mine, send = call(
        functools.partial(
            kernel,
            half,
            chan,
            tiles,
            2.0 * pref,
            2.0 * TWO_PI * pref / BOX,
            pref / atoms,
        ),
        1,
        (f32(result, 128), f32(result, 128)),
        (t_own, t_two, line, atom, load, counts, ends, second[0], across),
    )
    theirs = lax.ppermute(send, "wave", [(b, b ^ 1) for b in range(columns)])
    pot, force, energy = pl.pallas_call(
        functools.partial(join_kernel, half, chan),
        out_shape=(
            jax.ShapeDtypeStruct((frames, chan, 128), jnp.float32),
            jax.ShapeDtypeStruct((3, frames, 128), jnp.float32),
            jax.ShapeDtypeStruct((frames,), jnp.float32),
        ),
        in_specs=[VMEM, VMEM],
        out_specs=(VMEM, VMEM, SMEM),
        compiler_params=pltpu.CompilerParams(vmem_limit_bytes=4 * 2**20),
    )(mine, theirs)
    return pot, force.transpose(1, 0, 2), energy


def solution(mesh):
    return jax.shard_map(
        per_device,
        mesh=mesh,
        in_specs=(
            P(None, None, ("group", "atom")),
            P(None, None, ("group", "atom")),
            P(None, "wave"),
        ),
        out_specs=(
            P(None, None, ("group", "atom", "wave")),
            P(None, None, ("group", "atom", "wave")),
            P("group"),
        ),
        check_vma=False,
    )
```

```python
import functools
import math

import jax
import jax.numpy as jnp
from jax import lax
from jax.experimental import pallas as pl
from jax.experimental.pallas import tpu as pltpu
from jax.sharding import PartitionSpec as P

BOX = 32
TWO_PI = 2.0 * math.pi
GAUSS = 256.0
TOP = 8

SIN = (3.14159265, -5.16771008, 2.55007753, -0.59829131, 0.07765766)
COS = (1.0, -4.93479283, 4.05841139, -1.33187667, 0.21968962)

NT = (((1,), (1,)), ((), ()))
NN = (((1,), (0,)), ((), ()))
TN = (((0,), (0,)), ((), ()))


def horner(coefs, u):
    value = jnp.full_like(u, coefs[-1])
    for c in coefs[-2::-1]:
        value = value * u + c
    return value


def cos_sin(turns):
    r = turns - jnp.round(turns)
    u = r * r
    s = r * horner(SIN, u)
    c = horner(COS, u)
    return 1.0 - 2.0 * (s * s), 2.0 * (s * c)


def iota(shape, dim):
    return lax.broadcasted_iota(jnp.int32, shape, dim)


def bases(x, y, z):
    k = iota(x.shape, 0)
    kf = k.astype(jnp.float32)
    out = [cos_sin(kf * v) for v in (x, y, z)]
    last = jnp.where(k < 2, x, jnp.where(k < 4, y, z))
    quarter = jnp.where((k & 1) == 1, 0.25, 0.0)
    out.append(cos_sin(TOP * last - quarter))
    return out


def census(blocks, counts, ends):
    for block in blocks:
        n0, n1, n2 = block
        n = n0.shape[1]
        a0, a1, a2 = jnp.abs(n0), jnp.abs(n1), jnp.abs(n2)
        one = jnp.ones_like(n0)
        zero = jnp.zeros_like(n0)

        def sgn(v):
            return jnp.where(v > 0, one, jnp.where(v < 0, -one, zero))

        s0, s1, s2 = sgn(n0), sgn(n1), sgn(n2)
        row = iota((64, n), 0)
        key = ((row // 8) * 16 + row % 8).astype(jnp.float32)
        left = jnp.where(key == a0 * 16.0 + a1, 1.0, 0.0)
        row8 = iota((8, n), 0)
        k8 = row8.astype(jnp.float32)
        hit = k8 == a2
        right = jnp.concatenate(
            [jnp.where(hit, s, 0.0) for s in (one, s1 * s2, s0 * s2, s0 * s1)], 0
        )
        counts += lax.dot_general(
            left.astype(jnp.bfloat16),
            right.astype(jnp.bfloat16),
            NT,
            preferred_element_type=jnp.float32,
        )
        size = jnp.where(row8 < 2, a0, jnp.where(row8 < 4, a1, a2))
        end = jnp.where(size == TOP, 1.0, 0.0)
        for j in range(0, n, 128):
            ends += end[:, j : j + 128]
    return counts, ends


def weights(counts, ends):
    row = iota((64, 128), 0)
    lane = iota((64, 128), 1)
    k0, k1, k2 = row // 8, row % 8, (lane // 8) % 8
    square = (k0 * k0 + k1 * k1 + k2 * k2).astype(jnp.float32)
    some = square > 0
    safe = jnp.where(some, square, 1.0)
    gauss = jnp.where(some, jnp.exp(-safe / GAUSS) / safe, 0.0)
    source = iota((32, 128), 0)
    target = iota((32, 128), 1)
    tau = jnp.where(target < 64, 1.0, -1.0)
    out = []
    for v in range(4):
        pick = jnp.where(source == v * 8 + (target // 8) % 8, 1.0, 0.0)
        if v in (1, 2):
            pick = pick * tau
        spread = lax.dot_general(
            counts.astype(jnp.bfloat16),
            pick.astype(jnp.bfloat16),
            NN,
            preferred_element_type=jnp.float32,
        )
        out.append(gauss * spread)
    number = jnp.sum(ends, axis=1, keepdims=True)
    edge = math.exp(-TOP * TOP / GAUSS) / (TOP * TOP)
    keep = (iota((8, 128), 1) < 8) & (iota((8, 128), 0) < 6)
    return out, jnp.where(keep, edge * number, 0.0)


def spectrum(t, w, ends):
    tile = lambda j, y: t[16 * j + 8 * y : 16 * j + 8 * y + 8]
    turn = lambda v: pltpu.roll(v, 64, 1)
    out = []
    for k0 in range(8):
        w0, w1, w2, w3 = (v[8 * k0 : 8 * k0 + 8] for v in w)
        for x in range(2):
            if k0 == 0 and x == 1:
                out.append(ends * tile(1, 0))
                out.append(jnp.zeros_like(ends))
                continue
            for y in range(2):
                sy = 1.0 if y == 0 else -1.0
                sx = 1.0 if x == 0 else -1.0
                m = w0 * tile(2 * k0 + x, y) - sy * w1 * turn(tile(2 * k0 + x, 1 - y))
                if k0:
                    m = m - sx * w2 * turn(tile(2 * k0 + 1 - x, y))
                    m = m - sx * sy * w3 * tile(2 * k0 + 1 - x, 1 - y)
                out.append(m)
    return jnp.concatenate(out, 0)


def lines(block, first, tiles):
    return jnp.concatenate([block[first + t : first + t + 1] for t in range(tiles)], 1)


def tall(line):
    return jnp.broadcast_to(line, (8, line.shape[1]))


def pack_kernel(
    half, tiles, pos_hbm, charge_hbm, lattice_hbm, full_ref, own_ref, near_ref, pos_ref, charge_ref, lattice_ref, sem
):
    copies = [
        pltpu.make_async_copy(a, b, sem.at[i])
        for i, (a, b) in enumerate(
            ((charge_hbm, charge_ref), (pos_hbm, pos_ref), (lattice_hbm, lattice_ref))
        )
    ]
    for c in copies:
        c.start()
    for c in copies:
        c.wait()
    mine = lax.rem(lax.axis_index("wave"), 2)
    chan = charge_ref.shape[1]
    cut = lambda t: slice(128 * t, 128 * t + 128)
    row = 0
    for side, outs in ((mine, (full_ref, own_ref)), (1 - mine, (full_ref,))):
        for f in range(half):
            q = charge_ref[side * half + f].astype(jnp.float32)
            for t in range(tiles):
                for out in outs:
                    out[row : row + chan, :] = q[:, cut(t)]
                row += chan
        for f in range(half):
            for d in range(3):
                line = pos_ref[d, pl.ds(side * half + f, 1), :]
                for t in range(tiles):
                    for out in outs:
                        out[row : row + 1, :] = line[:, cut(t)]
                    row += 1
    near_ref[3 * tiles :, :] = jnp.zeros((near_ref.shape[0] - 3 * tiles, 128), jnp.float32)
    lattice = lattice_ref[...].astype(jnp.float32)
    for d in range(3):
        for t in range(tiles):
            row = d * tiles + t
            near_ref[row : row + 1, :] = lattice[d : d + 1, cut(t)]


def spread(ref, row):
    return tall(ref[pl.ds(row, 1), :])


def place(block, frame, first, picks):
    return [
        jnp.concatenate(
            [spread(block, first + (frame * 3 + d) * picks[0] + t) for t in picks[1]], 1
        )
        for d in range(3)
    ]


def fill(block, chan, tiles, half, frame, a_ref, b_ref, table, base):
    x, y, z = place(block, frame, half * tiles * chan, (tiles, range(tiles)))
    (xc, xs), (yc, ys), (zc, zs), (ec, _) = bases(x, y, z)
    q = jnp.concatenate(
        [block[pl.ds((frame * tiles + t) * chan, chan), :] for t in range(tiles)], 1
    )
    table[0:8] = xc
    table[8:16] = xs
    table[16:24] = zc
    table[24:32] = zs
    columns = pl.ds(base, 128 * tiles)
    for k0 in range(8):
        for kind in range(2):
            j = 2 * k0 + kind
            if j == 1:
                value = jnp.concatenate([ec, ec], 0)
            else:
                f = spread(table, 8 * kind + k0)
                value = jnp.concatenate([f * yc, f * ys], 0)
            a_ref[16 * j : 16 * j + 16, columns] = value.astype(jnp.bfloat16)
    for kind in range(2):
        for k in range(0, 8, 2):
            j = 8 * kind + k
            value = jnp.concatenate([spread(table, 16 + j) * q, spread(table, 17 + j) * q], 0)
            b_ref[8 * j : 8 * j + 16, columns] = value.astype(jnp.bfloat16)


def sums(blocks, rest, half, chan, tiles, frame, a_ref, b_ref, basis):
    width = 128 * tiles
    a, b = a_ref.at[frame % 2], b_ref.at[frame % 2]
    for slot, block in enumerate(blocks):
        fill(block, chan, tiles, half, frame, a, b, basis.at[slot % 2], slot * width)
    for ref in rest:

        @pl.loop(0, ref.shape[0])
        def _(i):
            base = pl.multiple_of((i + len(blocks)) * width, width)
            fill(ref.at[i], chan, tiles, half, frame, a, b, basis.at[0], base)

    return lax.dot_general(a[...], b[...], NT, preferred_element_type=jnp.float32)


def lattice_blocks(tiles, places):
    blocks = []
    for ref, at in places:
        v = ref[at : at + 3 * tiles, :]
        blocks.append([lines(v, d * tiles, tiles) for d in range(3)])
    return blocks


def count_kernel(tiles, near, beside, out_ref):
    zeros = jnp.zeros((64, 32), jnp.float32), jnp.zeros((8, 128), jnp.float32)
    counts, ends = census(lattice_blocks(tiles, ((near, 0), (beside, 0))), *zeros)
    out_ref[0:64] = jnp.concatenate([counts, jnp.zeros((64, 96), jnp.float32)], 1)
    out_ref[64:72] = ends


def pass_kernel(half, chan, tiles, count, *refs):
    u_ref, pieces = refs[0], refs[1 : 1 + count]
    t_ref, a_ref, b_ref, basis, block = refs[1 + count :]
    if count == 1:
        block = pieces[0]
    else:
        row = 0
        for piece in pieces:
            block[row : row + piece.shape[0], :] = piece[...]
            row += piece.shape[0]
    for frame in range(half):
        t_ref[frame] = u_ref[frame] + sums(
            (block,), (), half, chan, tiles, frame, a_ref, b_ref, basis
        )


def sums_kernel(half, chan, tiles, count, more, *refs):
    blocks, rest = refs[:count], refs[count : count + more]
    t_ref, a_ref, b_ref, basis = refs[count + more :]
    for frame in range(half):
        t_ref[frame] = sums(blocks, rest, half, chan, tiles, frame, a_ref, b_ref, basis)


def split(value):
    high = value.astype(jnp.bfloat16)
    return high, (value - high.astype(jnp.float32)).astype(jnp.bfloat16)


def early_kernel(half, chan, tiles, own, t_ref, line_ref, atom_ref, load_ref, a_ref, b_ref, basis):
    here = lax.axis_index("wave")
    pair = (here, here + 1 - 2 * lax.rem(here, 2))
    for frame in range(half):
        t_ref[frame] = sums((own,), (), half, chan, tiles, frame, a_ref, b_ref, basis)
        x, y, z = place(own, frame, half * tiles * chan, (tiles, pair))
        (xc, xs), (yc, ys), (zc, zs), (ec, es) = bases(x, y, z)
        q = jnp.concatenate(
            [
                own[pl.ds(pl.multiple_of((frame * tiles + p) * chan, chan), chan), :]
                for p in pair
            ],
            1,
        )
        line_ref[frame] = jnp.concatenate([xc, xs, yc, ys, zc, zs, es, q], 0)
        for k0 in range(8):
            for kind, x in enumerate((xc, xs)):
                f = tall(x[k0 : k0 + 1])
                if k0 == 0 and kind == 1:
                    value = jnp.concatenate([ec, jnp.zeros_like(ec)], 0)
                else:
                    value = jnp.concatenate([f * yc, f * ys], 0)
                at = 16 * (2 * k0 + kind)
                high, low = split(value)
                atom_ref[frame, 0, at : at + 16] = high
                atom_ref[frame, 1, at : at + 16] = low
        for kind, z in enumerate((zc, zs)):
            for k in range(0, 8, 2):
                value = jnp.concatenate([tall(z[k : k + 1]) * q, tall(z[k + 1 : k + 2]) * q], 0)
                at = 8 * (8 * kind + k)
                high, low = split(value)
                load_ref[frame, at : at + 16] = high
                load_ref[frame, 128 + at : 144 + at] = high
                load_ref[frame, 256 + at : 272 + at] = low


def kernel(half, chan, tiles, scale_pot, scale_force, scale_energy, *refs):
    t_ref, line_ref, atom_ref, load_ref, beside, across, mine_ref, send_ref = refs[:8]
    tally = beside[0:72, :] + across[0:72, :]
    w, ends = weights(tally[0:64, 0:32], tally[64:72])
    dot = functools.partial(lax.dot_general, preferred_element_type=jnp.float32)
    ts = [t_ref[frame] for frame in range(half)]
    ms = [spectrum(t, w, ends) for t in ts]
    backs, outs = [], []
    for frame in range(half):
        high, low = split(ms[frame])
        backs.append(
            dot(jnp.concatenate([high, low], 1), load_ref[frame, 0:256], NN)
            + dot(high, load_ref[frame, 256:384], NN)
        )
        outs.append(
            dot(high, atom_ref[frame, 0], TN)
            + dot(high, atom_ref[frame, 1], TN)
            + dot(low, atom_ref[frame, 0], TN)
        )
    for frame in range(half):
        energy = scale_energy * jnp.sum(
            jnp.sum(ts[frame] * ms[frame], 0, keepdims=True), 1, keepdims=True
        )
        h, u = backs[frame], outs[frame]
        xc, xs, yc, ys, zc, zs, es, q = (line_ref[frame, 8 * i : 8 * i + 8] for i in range(8))
        row = lambda v, k: jnp.broadcast_to(v[k : k + 1], v.shape)
        xrow = [(row(xc, k), row(xs, k)) for k in range(8)]
        zrow = [[row(v, k) for k in range(8)] for v in (zc, zs)]
        pot = jnp.zeros_like(q)
        dz = jnp.zeros_like(q)
        for k in range(8):
            uc = u[8 * k : 8 * k + 8]
            us = u[64 + 8 * k : 72 + 8 * k]
            pot = pot + zrow[0][k] * uc + zrow[1][k] * us
            if k:
                dz = dz + float(k) * (zrow[0][k] * us - zrow[1][k] * uc)
        dx = jnp.zeros_like(q)
        gc = jnp.zeros_like(q)
        gs = jnp.zeros_like(q)
        for k0 in range(8):
            parts = []
            for kind in range(2):
                if k0 == 0 and kind == 1:
                    continue
                j = 2 * k0 + kind
                hc = h[16 * j : 16 * j + 8]
                hs = h[16 * j + 8 : 16 * j + 16]
                parts.append(hc * yc + hs * ys)
                gc = gc + xrow[k0][kind] * hc
                gs = gs + xrow[k0][kind] * hs
            if k0:
                dx = dx + float(k0) * (xrow[k0][0] * parts[1] - xrow[k0][1] * parts[0])
        k1 = iota(q.shape, 0).astype(jnp.float32)
        dy = k1 * (yc * gs - ys * gc)
        edge = -float(TOP) * es * h[16:24]
        total = lambda v: jnp.sum(v, axis=0, keepdims=True)
        fx = total(dx) + edge[0:1] + edge[1:2]
        fy = total(dy) + edge[2:3] + edge[3:4]
        fz = total(dz * q) + edge[4:5] + edge[5:6]
        pot = scale_pot * pot
        forces = [-scale_force * v for v in (fx, fy, fz)]
        for out, cut in ((mine_ref, slice(0, 128)), (send_ref, slice(128, 256))):
            out[chan * frame : chan * frame + chan, :] = pot[:, cut]
            for d in range(3):
                at = half * chan + 3 * frame + d
                out[at : at + 1, :] = forces[d][:, cut]
            at = half * (chan + 3) + frame
            out[at : at + 1, :] = jnp.broadcast_to(energy, (1, 128))


def join_kernel(half, chan, mine_ref, theirs_ref, pot_ref, force_ref, energy_ref):
    side = lax.rem(lax.axis_index("wave"), 2)
    for ref, which in ((mine_ref, side), (theirs_ref, 1 - side)):
        for f in range(half):
            to = which * half + f
            pot_ref[to] = ref[chan * f : chan * f + chan, :]
            for d in range(3):
                at = half * chan + 3 * f + d
                force_ref[d, pl.ds(to, 1), :] = ref[at : at + 1, :]
            energy_ref[to] = ref[half * (chan + 3) + f, 0]


COST = 1
VMEM = pl.BlockSpec(memory_space=pltpu.VMEM)
SMEM = pl.BlockSpec(memory_space=pltpu.SMEM)


def per_device(positions, charges, lattice):
    frames, chan, width = charges.shape
    rows, columns = lax.axis_size("atom"), lax.axis_size("wave")
    atoms = width * rows
    pref = 1.0 / math.sqrt(atoms)
    half = frames // 2
    tiles = width // 128
    assert width // columns == 128 and columns == 4 and rows % 4 == 0
    size = half * tiles * (chan + 3)
    hbm = pl.BlockSpec(memory_space=pltpu.HBM)
    full, own, near = pl.pallas_call(
        functools.partial(pack_kernel, half, tiles),
        out_shape=(
            jax.ShapeDtypeStruct((2 * size, 128), jnp.float32),
            jax.ShapeDtypeStruct((size, 128), jnp.float32),
            jax.ShapeDtypeStruct((32, 128), jnp.float32),
        ),
        in_specs=[hbm] * 3,
        out_specs=(VMEM, VMEM, VMEM),
        scratch_shapes=[
            pltpu.VMEM((3, frames, width), jnp.float32),
            pltpu.VMEM((frames, chan, width), jnp.bfloat16),
            pltpu.VMEM((3, width), jnp.int32),
            pltpu.SemaphoreType.DMA((3,)),
        ],
        compiler_params=pltpu.CompilerParams(vmem_limit_bytes=4 * 2**20),
    )(
        *(
            pltpu.with_memory_space_constraint(v, pltpu.HBM)
            for v in (positions.transpose(1, 0, 2), charges, lattice)
        )
    )

    def send_to(value, target):
        pairs = []
        for a in range(rows):
            for b in range(columns):
                to, on = target(a, b)
                pairs.append((a * columns + b, to * columns + on))
        return lax.ppermute(value, ("atom", "wave"), pairs)

    first = send_to(full, lambda a, b: (a ^ (1 + b % 2), b))
    second = [send_to(own, lambda a, b, k=k: (a ^ k, b)) for k in range(3, rows)]
    scratch = lambda n: [
        pltpu.VMEM((2, 256, n), jnp.bfloat16),
        pltpu.VMEM((2, 128, n), jnp.bfloat16),
        pltpu.VMEM((2, 32, width), jnp.float32),
    ]

    f32 = lambda *shape: jax.ShapeDtypeStruct(shape, jnp.float32)
    bf16 = lambda *shape: jax.ShapeDtypeStruct(shape, jnp.bfloat16)

    def call(body, blocks, out_shape, args, limit=8, more=()):
        return pl.pallas_call(
            body,
            out_shape=out_shape,
            in_specs=[VMEM] * len(args),
            out_specs=tuple(VMEM for _ in out_shape),
            scratch_shapes=scratch(width * blocks) + list(more),
            compiler_params=pltpu.CompilerParams(vmem_limit_bytes=limit * 2**20),
            cost_estimate=pl.CostEstimate(
                flops=COST, bytes_accessed=COST, transcendentals=0
            ),
        )(*args)

    totals = f32(half, 256, 128)
    t_own, line, atom, load = call(
        functools.partial(early_kernel, half, chan, tiles),
        1,
        (totals, f32(half, 64, 256), bf16(half, 2, 256, 256), bf16(half, 384, 256)),
        (own,),
    )
    beside = lax.ppermute(near, "wave", [(b, b ^ 1) for b in range(columns)])
    both = pl.pallas_call(
        functools.partial(count_kernel, tiles),
        out_shape=jax.ShapeDtypeStruct((72, 128), jnp.float32),
        in_specs=[VMEM] * 2,
        out_specs=VMEM,
        compiler_params=pltpu.CompilerParams(vmem_limit_bytes=4 * 2**20),
        cost_estimate=pl.CostEstimate(flops=COST, bytes_accessed=COST, transcendentals=0),
    )(near, beside)
    across = lax.ppermute(both, "wave", [(b, b ^ 2) for b in range(columns)])
    first, both = lax.optimization_barrier((first, both))
    middle = size + half * tiles * chan
    passed = [
        lax.ppermute(piece, "wave", [(b, b ^ 1) for b in range(columns)])
        for piece in (first[size:middle], first[middle:])
    ]
    t_sum = t_own
    for block in ([first], passed, second[:1]):
        (t_sum,) = call(
            functools.partial(pass_kernel, half, chan, tiles, len(block)),
            1,
            (totals,),
            (t_sum, *block),
            more=[pltpu.VMEM((size, 128), jnp.float32)],
        )
    if rows > 4:
        (t_rest,) = call(
            functools.partial(sums_kernel, half, chan, tiles, 0, 1),
            rows - 4,
            (totals,),
            (jnp.stack(second[1:]),),
            40,
        )
        t_sum = t_sum + t_rest
    result = -(-half * (chan + 4) // 8) * 8
    mine, send = call(
        functools.partial(
            kernel,
            half,
            chan,
            tiles,
            2.0 * pref,
            2.0 * TWO_PI * pref / BOX,
            pref / atoms,
        ),
        1,
        (f32(result, 128), f32(result, 128)),
        (t_sum, line, atom, load, both, across),
    )
    theirs = lax.ppermute(send, "wave", [(b, b ^ 1) for b in range(columns)])
    pot, force, energy = pl.pallas_call(
        functools.partial(join_kernel, half, chan),
        out_shape=(
            jax.ShapeDtypeStruct((frames, chan, 128), jnp.float32),
            jax.ShapeDtypeStruct((3, frames, 128), jnp.float32),
            jax.ShapeDtypeStruct((frames,), jnp.float32),
        ),
        in_specs=[VMEM, VMEM],
        out_specs=(VMEM, VMEM, SMEM),
        compiler_params=pltpu.CompilerParams(vmem_limit_bytes=4 * 2**20),
    )(mine, theirs)
    return pot, force.transpose(1, 0, 2), energy


def solution(mesh):
    return jax.shard_map(
        per_device,
        mesh=mesh,
        in_specs=(
            P(None, None, ("group", "atom")),
            P(None, None, ("group", "atom")),
            P(None, "wave"),
        ),
        out_specs=(
            P(None, None, ("group", "atom", "wave")),
            P(None, None, ("group", "atom", "wave")),
            P("group"),
        ),
        check_vma=False,
    )
```

```python
import functools
import math

import jax
import jax.numpy as jnp
from jax import lax
from jax.experimental import pallas as pl
from jax.experimental.pallas import tpu as pltpu
from jax.sharding import PartitionSpec as P

BOX = 32
TWO_PI = 2.0 * math.pi
GAUSS = 256.0
TOP = 8

SIN = (3.14159265, -5.16771008, 2.55007753, -0.59829131, 0.07765766)
COS = (1.0, -4.93479283, 4.05841139, -1.33187667, 0.21968962)

NT = (((1,), (1,)), ((), ()))
NN = (((1,), (0,)), ((), ()))
TN = (((0,), (0,)), ((), ()))


def horner(coefs, u):
    value = jnp.full_like(u, coefs[-1])
    for c in coefs[-2::-1]:
        value = value * u + c
    return value


def cos_sin(turns):
    r = turns - jnp.round(turns)
    u = r * r
    s = r * horner(SIN, u)
    c = horner(COS, u)
    return 1.0 - 2.0 * (s * s), 2.0 * (s * c)


def iota(shape, dim):
    return lax.broadcasted_iota(jnp.int32, shape, dim)


def bases(x, y, z):
    k = iota(x.shape, 0)
    kf = k.astype(jnp.float32)
    out = [cos_sin(kf * v) for v in (x, y, z)]
    last = jnp.where(k < 2, x, jnp.where(k < 4, y, z))
    quarter = jnp.where((k & 1) == 1, 0.25, 0.0)
    out.append(cos_sin(TOP * last - quarter))
    return out


def census(blocks, counts, ends):
    for block in blocks:
        n0, n1, n2 = block
        n = n0.shape[1]
        a0, a1, a2 = jnp.abs(n0), jnp.abs(n1), jnp.abs(n2)
        one = jnp.ones_like(n0)
        zero = jnp.zeros_like(n0)

        def sgn(v):
            return jnp.where(v > 0, one, jnp.where(v < 0, -one, zero))

        s0, s1, s2 = sgn(n0), sgn(n1), sgn(n2)
        row = iota((64, n), 0)
        key = ((row // 8) * 16 + row % 8).astype(jnp.float32)
        left = jnp.where(key == a0 * 16.0 + a1, 1.0, 0.0)
        row8 = iota((8, n), 0)
        k8 = row8.astype(jnp.float32)
        hit = k8 == a2
        right = jnp.concatenate(
            [jnp.where(hit, s, 0.0) for s in (one, s1 * s2, s0 * s2, s0 * s1)], 0
        )
        counts += lax.dot_general(
            left.astype(jnp.bfloat16),
            right.astype(jnp.bfloat16),
            NT,
            preferred_element_type=jnp.float32,
        )
        size = jnp.where(row8 < 2, a0, jnp.where(row8 < 4, a1, a2))
        end = jnp.where(size == TOP, 1.0, 0.0)
        for j in range(0, n, 128):
            ends += end[:, j : j + 128]
    return counts, ends


def weights(counts, ends):
    row = iota((64, 128), 0)
    lane = iota((64, 128), 1)
    k0, k1, k2 = row // 8, row % 8, (lane // 8) % 8
    square = (k0 * k0 + k1 * k1 + k2 * k2).astype(jnp.float32)
    some = square > 0
    safe = jnp.where(some, square, 1.0)
    gauss = jnp.where(some, jnp.exp(-safe / GAUSS) / safe, 0.0)
    source = iota((32, 128), 0)
    target = iota((32, 128), 1)
    tau = jnp.where(target < 64, 1.0, -1.0)
    out = []
    for v in range(4):
        pick = jnp.where(source == v * 8 + (target // 8) % 8, 1.0, 0.0)
        if v in (1, 2):
            pick = pick * tau
        spread = lax.dot_general(
            counts.astype(jnp.bfloat16),
            pick.astype(jnp.bfloat16),
            NN,
            preferred_element_type=jnp.float32,
        )
        out.append(gauss * spread)
    number = jnp.sum(ends, axis=1, keepdims=True)
    edge = math.exp(-TOP * TOP / GAUSS) / (TOP * TOP)
    keep = (iota((8, 128), 1) < 8) & (iota((8, 128), 0) < 6)
    return out, jnp.where(keep, edge * number, 0.0)


def spectrum(t, w, ends):
    tile = lambda j, y: t[16 * j + 8 * y : 16 * j + 8 * y + 8]
    turn = lambda v: pltpu.roll(v, 64, 1)
    out = []
    for k0 in range(8):
        w0, w1, w2, w3 = (v[8 * k0 : 8 * k0 + 8] for v in w)
        for x in range(2):
            if k0 == 0 and x == 1:
                out.append(ends * tile(1, 0))
                out.append(jnp.zeros_like(ends))
                continue
            for y in range(2):
                sy = 1.0 if y == 0 else -1.0
                sx = 1.0 if x == 0 else -1.0
                m = w0 * tile(2 * k0 + x, y) - sy * w1 * turn(tile(2 * k0 + x, 1 - y))
                if k0:
                    m = m - sx * w2 * turn(tile(2 * k0 + 1 - x, y))
                    m = m - sx * sy * w3 * tile(2 * k0 + 1 - x, 1 - y)
                out.append(m)
    return jnp.concatenate(out, 0)


def lines(block, first, tiles):
    return jnp.concatenate([block[first + t : first + t + 1] for t in range(tiles)], 1)


def tall(line):
    return jnp.broadcast_to(line, (8, line.shape[1]))


def pack_kernel(
    half, tiles, pos_hbm, charge_hbm, lattice_hbm, full_ref, own_ref, near_ref, pos_ref, charge_ref, lattice_ref, sem
):
    copies = [
        pltpu.make_async_copy(a, b, sem.at[i])
        for i, (a, b) in enumerate(
            ((charge_hbm, charge_ref), (pos_hbm, pos_ref), (lattice_hbm, lattice_ref))
        )
    ]
    for c in copies:
        c.start()
    for c in copies:
        c.wait()
    mine = lax.rem(lax.axis_index("wave"), 2)
    chan = charge_ref.shape[1]
    cut = lambda t: slice(128 * t, 128 * t + 128)
    row = 0
    for side, outs in ((mine, (full_ref, own_ref)), (1 - mine, (full_ref,))):
        for f in range(half):
            q = charge_ref[side * half + f].astype(jnp.float32)
            for t in range(tiles):
                for out in outs:
                    out[row : row + chan, :] = q[:, cut(t)]
                row += chan
        for f in range(half):
            for d in range(3):
                line = pos_ref[d, pl.ds(side * half + f, 1), :]
                for t in range(tiles):
                    for out in outs:
                        out[row : row + 1, :] = line[:, cut(t)]
                    row += 1
    near_ref[3 * tiles :, :] = jnp.zeros((near_ref.shape[0] - 3 * tiles, 128), jnp.float32)
    lattice = lattice_ref[...].astype(jnp.float32)
    for d in range(3):
        for t in range(tiles):
            row = d * tiles + t
            near_ref[row : row + 1, :] = lattice[d : d + 1, cut(t)]


def spread(ref, row):
    return tall(ref[pl.ds(row, 1), :])


def place(block, frame, first, picks):
    return [
        jnp.concatenate(
            [spread(block, first + (frame * 3 + d) * picks[0] + t) for t in picks[1]], 1
        )
        for d in range(3)
    ]


def fill(block, chan, tiles, half, frame, a_ref, b_ref, table, base):
    x, y, z = place(block, frame, half * tiles * chan, (tiles, range(tiles)))
    (xc, xs), (yc, ys), (zc, zs), (ec, _) = bases(x, y, z)
    q = jnp.concatenate(
        [block[pl.ds((frame * tiles + t) * chan, chan), :] for t in range(tiles)], 1
    )
    table[0:8] = xc
    table[8:16] = xs
    table[16:24] = zc
    table[24:32] = zs
    columns = pl.ds(base, 128 * tiles)
    for k0 in range(8):
        for kind in range(2):
            j = 2 * k0 + kind
            if j == 1:
                value = jnp.concatenate([ec, ec], 0)
            else:
                f = spread(table, 8 * kind + k0)
                value = jnp.concatenate([f * yc, f * ys], 0)
            a_ref[16 * j : 16 * j + 16, columns] = value.astype(jnp.bfloat16)
    for kind in range(2):
        for k in range(0, 8, 2):
            j = 8 * kind + k
            value = jnp.concatenate([spread(table, 16 + j) * q, spread(table, 17 + j) * q], 0)
            b_ref[8 * j : 8 * j + 16, columns] = value.astype(jnp.bfloat16)


def sums(blocks, rest, half, chan, tiles, frame, a_ref, b_ref, basis):
    width = 128 * tiles
    a, b = a_ref.at[frame % 2], b_ref.at[frame % 2]
    for slot, block in enumerate(blocks):
        fill(block, chan, tiles, half, frame, a, b, basis.at[slot % 2], slot * width)
    for ref in rest:

        @pl.loop(0, ref.shape[0])
        def _(i):
            base = pl.multiple_of((i + len(blocks)) * width, width)
            fill(ref.at[i], chan, tiles, half, frame, a, b, basis.at[0], base)

    return lax.dot_general(a[...], b[...], NT, preferred_element_type=jnp.float32)


def lattice_blocks(tiles, places):
    blocks = []
    for ref, at in places:
        v = ref[at : at + 3 * tiles, :]
        blocks.append([lines(v, d * tiles, tiles) for d in range(3)])
    return blocks


def count_kernel(tiles, near, beside, out_ref):
    zeros = jnp.zeros((64, 32), jnp.float32), jnp.zeros((8, 128), jnp.float32)
    counts, ends = census(lattice_blocks(tiles, ((near, 0), (beside, 0))), *zeros)
    out_ref[0:64] = jnp.concatenate([counts, jnp.zeros((64, 96), jnp.float32)], 1)
    out_ref[64:72] = ends


def pass_kernel(half, chan, tiles, count, *refs):
    u_ref, pieces = refs[0], refs[1 : 1 + count]
    t_ref, a_ref, b_ref, basis, block = refs[1 + count :]
    if count == 1:
        block = pieces[0]
    else:
        row = 0
        for piece in pieces:
            block[row : row + piece.shape[0], :] = piece[...]
            row += piece.shape[0]
    for frame in range(half):
        t_ref[frame] = u_ref[frame] + sums(
            (block,), (), half, chan, tiles, frame, a_ref, b_ref, basis
        )


def sums_kernel(half, chan, tiles, count, more, *refs):
    blocks, rest = refs[:count], refs[count : count + more]
    t_ref, a_ref, b_ref, basis = refs[count + more :]
    for frame in range(half):
        t_ref[frame] = sums(blocks, rest, half, chan, tiles, frame, a_ref, b_ref, basis)


def split(value):
    high = value.astype(jnp.bfloat16)
    return high, (value - high.astype(jnp.float32)).astype(jnp.bfloat16)


def early_kernel(half, chan, tiles, own, t_ref, line_ref, atom_ref, load_ref, a_ref, b_ref, basis):
    here = lax.axis_index("wave")
    pair = (here, here + 1 - 2 * lax.rem(here, 2))
    for frame in range(half):
        t_ref[frame] = sums((own,), (), half, chan, tiles, frame, a_ref, b_ref, basis)
        x, y, z = place(own, frame, half * tiles * chan, (tiles, pair))
        (xc, xs), (yc, ys), (zc, zs), (ec, es) = bases(x, y, z)
        q = jnp.concatenate(
            [
                own[pl.ds(pl.multiple_of((frame * tiles + p) * chan, chan), chan), :]
                for p in pair
            ],
            1,
        )
        line_ref[frame] = jnp.concatenate([xc, xs, yc, ys, zc, zs, es, q], 0)
        for k0 in range(8):
            for kind, x in enumerate((xc, xs)):
                f = tall(x[k0 : k0 + 1])
                if k0 == 0 and kind == 1:
                    value = jnp.concatenate([ec, jnp.zeros_like(ec)], 0)
                else:
                    value = jnp.concatenate([f * yc, f * ys], 0)
                at = 16 * (2 * k0 + kind)
                high, low = split(value)
                atom_ref[frame, 0, at : at + 16] = high
                atom_ref[frame, 1, at : at + 16] = low
        for kind, z in enumerate((zc, zs)):
            for k in range(0, 8, 2):
                value = jnp.concatenate([tall(z[k : k + 1]) * q, tall(z[k + 1 : k + 2]) * q], 0)
                at = 8 * (8 * kind + k)
                high, low = split(value)
                load_ref[frame, at : at + 16] = high
                load_ref[frame, 128 + at : 144 + at] = high
                load_ref[frame, 256 + at : 272 + at] = low


def results(half, chan, scales, frame, high, low, lanes, line_ref, atom_ref, load_ref, out):
    scale_pot, scale_force = scales
    dot = functools.partial(lax.dot_general, preferred_element_type=jnp.float32)
    h = dot(jnp.concatenate([high, low], 1), load_ref[frame, 0:256, lanes], NN)
    h = h + dot(high, load_ref[frame, 256:384, lanes], NN)
    u = dot(high, atom_ref[frame, 0, :, lanes], TN)
    u = u + dot(high, atom_ref[frame, 1, :, lanes], TN)
    u = u + dot(low, atom_ref[frame, 0, :, lanes], TN)
    xc, xs, yc, ys, zc, zs, es, q = (
        line_ref[frame, 8 * i : 8 * i + 8, lanes] for i in range(8)
    )
    row = lambda v, k: jnp.broadcast_to(v[k : k + 1], v.shape)
    xrow = [(row(xc, k), row(xs, k)) for k in range(8)]
    zrow = [[row(v, k) for k in range(8)] for v in (zc, zs)]
    pot = jnp.zeros_like(q)
    dz = jnp.zeros_like(q)
    for k in range(8):
        uc = u[8 * k : 8 * k + 8]
        us = u[64 + 8 * k : 72 + 8 * k]
        pot = pot + zrow[0][k] * uc + zrow[1][k] * us
        if k:
            dz = dz + float(k) * (zrow[0][k] * us - zrow[1][k] * uc)
    dx = jnp.zeros_like(q)
    gc = jnp.zeros_like(q)
    gs = jnp.zeros_like(q)
    for k0 in range(8):
        parts = []
        for kind in range(2):
            if k0 == 0 and kind == 1:
                continue
            j = 2 * k0 + kind
            hc = h[16 * j : 16 * j + 8]
            hs = h[16 * j + 8 : 16 * j + 16]
            parts.append(hc * yc + hs * ys)
            gc = gc + xrow[k0][kind] * hc
            gs = gs + xrow[k0][kind] * hs
        if k0:
            dx = dx + float(k0) * (xrow[k0][0] * parts[1] - xrow[k0][1] * parts[0])
    k1 = iota(q.shape, 0).astype(jnp.float32)
    dy = k1 * (yc * gs - ys * gc)
    edge = -float(TOP) * es * h[16:24]
    total = lambda v: jnp.sum(v, axis=0, keepdims=True)
    fx = total(dx) + edge[0:1] + edge[1:2]
    fy = total(dy) + edge[2:3] + edge[3:4]
    fz = total(dz * q) + edge[4:5] + edge[5:6]
    pot = scale_pot * pot
    forces = [-scale_force * v for v in (fx, fy, fz)]
    out[chan * frame : chan * frame + chan, :] = pot
    for d in range(3):
        at = half * chan + 3 * frame + d
        out[at : at + 1, :] = forces[d]


def kernel(half, chan, scales, scale_energy, *refs):
    t_ref, line_ref, atom_ref, load_ref, beside, across, send_ref, m_ref = refs[:8]
    tally = beside[0:72, :] + across[0:72, :]
    w, ends = weights(tally[0:64, 0:32], tally[64:72])
    ts = [t_ref[frame] for frame in range(half)]
    ms = [spectrum(t, w, ends) for t in ts]
    tables = (slice(128, 256), line_ref, atom_ref, load_ref)
    for frame in range(half):
        high, low = split(ms[frame])
        m_ref[frame, 0] = high
        m_ref[frame, 1] = low
        results(half, chan, scales, frame, high, low, *tables, send_ref)
        energy = scale_energy * jnp.sum(
            jnp.sum(ts[frame] * ms[frame], 0, keepdims=True), 1, keepdims=True
        )
        at = half * (chan + 3) + frame
        send_ref[at : at + 1, :] = jnp.broadcast_to(energy, (1, 128))


def own_results_kernel(half, chan, scales, *refs):
    m_ref, send_ref, line_ref, atom_ref, load_ref, mine_ref = refs[:6]
    tables = (slice(0, 128), line_ref, atom_ref, load_ref)
    for frame in range(half):
        results(half, chan, scales, frame, m_ref[frame, 0], m_ref[frame, 1], *tables, mine_ref)
    at = half * (chan + 3)
    mine_ref[at : at + half, :] = send_ref[at : at + half, :]


def join_kernel(half, chan, mine_ref, theirs_ref, pot_ref, force_ref, energy_ref):
    side = lax.rem(lax.axis_index("wave"), 2)
    for ref, which in ((mine_ref, side), (theirs_ref, 1 - side)):
        for f in range(half):
            to = which * half + f
            pot_ref[to] = ref[chan * f : chan * f + chan, :]
            for d in range(3):
                at = half * chan + 3 * f + d
                force_ref[d, pl.ds(to, 1), :] = ref[at : at + 1, :]
            energy_ref[to] = ref[half * (chan + 3) + f, 0]


COST = 1
VMEM = pl.BlockSpec(memory_space=pltpu.VMEM)
SMEM = pl.BlockSpec(memory_space=pltpu.SMEM)


def per_device(positions, charges, lattice):
    frames, chan, width = charges.shape
    rows, columns = lax.axis_size("atom"), lax.axis_size("wave")
    atoms = width * rows
    pref = 1.0 / math.sqrt(atoms)
    half = frames // 2
    tiles = width // 128
    assert width // columns == 128 and columns == 4 and rows % 4 == 0
    size = half * tiles * (chan + 3)
    hbm = pl.BlockSpec(memory_space=pltpu.HBM)
    full, own, near = pl.pallas_call(
        functools.partial(pack_kernel, half, tiles),
        out_shape=(
            jax.ShapeDtypeStruct((2 * size, 128), jnp.float32),
            jax.ShapeDtypeStruct((size, 128), jnp.float32),
            jax.ShapeDtypeStruct((32, 128), jnp.float32),
        ),
        in_specs=[hbm] * 3,
        out_specs=(VMEM, VMEM, VMEM),
        scratch_shapes=[
            pltpu.VMEM((3, frames, width), jnp.float32),
            pltpu.VMEM((frames, chan, width), jnp.bfloat16),
            pltpu.VMEM((3, width), jnp.int32),
            pltpu.SemaphoreType.DMA((3,)),
        ],
        compiler_params=pltpu.CompilerParams(vmem_limit_bytes=4 * 2**20),
    )(
        *(
            pltpu.with_memory_space_constraint(v, pltpu.HBM)
            for v in (positions.transpose(1, 0, 2), charges, lattice)
        )
    )

    def send_to(value, target):
        pairs = []
        for a in range(rows):
            for b in range(columns):
                to, on = target(a, b)
                pairs.append((a * columns + b, to * columns + on))
        return lax.ppermute(value, ("atom", "wave"), pairs)

    first = send_to(full, lambda a, b: (a ^ (1 + b % 2), b))
    second = [send_to(own, lambda a, b, k=k: (a ^ k, b)) for k in range(3, rows)]
    scratch = lambda n: [
        pltpu.VMEM((2, 256, n), jnp.bfloat16),
        pltpu.VMEM((2, 128, n), jnp.bfloat16),
        pltpu.VMEM((2, 32, width), jnp.float32),
    ]

    f32 = lambda *shape: jax.ShapeDtypeStruct(shape, jnp.float32)
    bf16 = lambda *shape: jax.ShapeDtypeStruct(shape, jnp.bfloat16)

    def call(body, blocks, out_shape, args, limit=8, more=()):
        return pl.pallas_call(
            body,
            out_shape=out_shape,
            in_specs=[VMEM] * len(args),
            out_specs=tuple(VMEM for _ in out_shape),
            scratch_shapes=scratch(width * blocks) + list(more),
            compiler_params=pltpu.CompilerParams(vmem_limit_bytes=limit * 2**20),
            cost_estimate=pl.CostEstimate(
                flops=COST, bytes_accessed=COST, transcendentals=0
            ),
        )(*args)

    totals = f32(half, 256, 128)
    t_own, line, atom, load = call(
        functools.partial(early_kernel, half, chan, tiles),
        1,
        (totals, f32(half, 64, 256), bf16(half, 2, 256, 256), bf16(half, 384, 256)),
        (own,),
    )
    beside = lax.ppermute(near, "wave", [(b, b ^ 1) for b in range(columns)])
    both = pl.pallas_call(
        functools.partial(count_kernel, tiles),
        out_shape=jax.ShapeDtypeStruct((72, 128), jnp.float32),
        in_specs=[VMEM] * 2,
        out_specs=VMEM,
        compiler_params=pltpu.CompilerParams(vmem_limit_bytes=4 * 2**20),
        cost_estimate=pl.CostEstimate(flops=COST, bytes_accessed=COST, transcendentals=0),
    )(near, beside)
    across = lax.ppermute(both, "wave", [(b, b ^ 2) for b in range(columns)])
    first, both = lax.optimization_barrier((first, both))
    middle = size + half * tiles * chan
    passed = [
        lax.ppermute(piece, "wave", [(b, b ^ 1) for b in range(columns)])
        for piece in (first[size:middle], first[middle:])
    ]
    t_sum = t_own
    for block in ([first], passed, second[:1]):
        (t_sum,) = call(
            functools.partial(pass_kernel, half, chan, tiles, len(block)),
            1,
            (totals,),
            (t_sum, *block),
            more=[pltpu.VMEM((size, 128), jnp.float32)],
        )
    if rows > 4:
        (t_rest,) = call(
            functools.partial(sums_kernel, half, chan, tiles, 0, 1),
            rows - 4,
            (totals,),
            (jnp.stack(second[1:]),),
            40,
        )
        t_sum = t_sum + t_rest
    result = -(-half * (chan + 4) // 8) * 8
    scales = (2.0 * pref, 2.0 * TWO_PI * pref / BOX)
    send, m = call(
        functools.partial(kernel, half, chan, scales, pref / atoms),
        1,
        (f32(result, 128), bf16(half, 2, 256, 128)),
        (t_sum, line, atom, load, both, across),
    )
    theirs = lax.ppermute(send, "wave", [(b, b ^ 1) for b in range(columns)])
    (mine,) = call(
        functools.partial(own_results_kernel, half, chan, scales),
        1,
        (f32(result, 128),),
        (m, send, line, atom, load),
    )
    pot, force, energy = pl.pallas_call(
        functools.partial(join_kernel, half, chan),
        out_shape=(
            jax.ShapeDtypeStruct((frames, chan, 128), jnp.float32),
            jax.ShapeDtypeStruct((3, frames, 128), jnp.float32),
            jax.ShapeDtypeStruct((frames,), jnp.float32),
        ),
        in_specs=[VMEM, VMEM],
        out_specs=(VMEM, VMEM, SMEM),
        compiler_params=pltpu.CompilerParams(vmem_limit_bytes=4 * 2**20),
    )(mine, theirs)
    return pot, force.transpose(1, 0, 2), energy


def solution(mesh):
    return jax.shard_map(
        per_device,
        mesh=mesh,
        in_specs=(
            P(None, None, ("group", "atom")),
            P(None, None, ("group", "atom")),
            P(None, "wave"),
        ),
        out_specs=(
            P(None, None, ("group", "atom", "wave")),
            P(None, None, ("group", "atom", "wave")),
            P("group"),
        ),
        check_vma=False,
    )
```
